32 devices in a mesh: row: 8 (over z, core), col: 4 (over y, x).
Axes of the slice: x: 2, y: 2, z: 4, core: 2. Of those that a mesh axis runs over, the one named last changes fastest.
Arguments:
- queries: bfloat16 [512, 8192], P('col', 'row'), may hold values from -8 to 8
- cache_keys: bfloat16 [8, 32768, 128], P(None, ('row', 'col')), may hold values from -8 to 8
- cache_values: bfloat16 [8, 32768, 128], P(None, ('row', 'col')), may hold values from -6 to 6
- stretch_keys: bfloat16 [8, 512, 128], P(None, 'col'), may hold values from -8 to 8
- stretch_values: bfloat16 [8, 512, 128], P(None, 'col'), may hold values from -6 to 6
- block_lists: int32 [4, 8, 16], replicated, may hold values from 0 to 255, as said below
- out_weight: bfloat16 [8192, 8192], P('row', 'col'), may hold values from -0.5 to 0.5
- residual: bfloat16 [512, 8192], P('row', 'col'), may hold values from -6 to 6
- norm_gain: bfloat16 [8192], P('col'), may hold values from 0.25 to 1.75
- gate_weight: bfloat16 [8192, 28672], P('col', 'row'), may hold values from -0.0625 to 0.0625
- up_weight: bfloat16 [8192, 28672], P('col', 'row'), may hold values from -0.0625 to 0.0625
- down_weight: bfloat16 [28672, 8192], P('row', 'col'), may hold values from -0.03125 to 0.03125
Outputs:
- layer_out: bfloat16 [512, 8192], P('row', 'col')
The draws below stay inside these ranges and needn't reach their ends.
Inputs may be any that keep to these rules, and one draw needn't show every extreme that they name: `block_lists`: each list names 16 different cache blocks; device k of row+col holds cache blocks k * (8) to (k + 1) * 8 - 1, and no two blocks of one list lie on the same device. Every list holds block 0 and block 255.
All inputs are finite; a program needn't handle non-finite values.
Results may differ from the reference program's by a relative error of at most 0.0085.
Values may be sent and summed in bfloat16 or wider, within the bound.
A program may use at most 128 MiB of HBM per device.

```python
import math
import jax
import jax.numpy as jnp
from jax import lax

D = 8192
FF = 28672
HEADS = 64
KV_HEADS = 8
HEAD_DIM = 128
BLK = 128
CTX_DEV = 1024
NSEL = 16
GROUP = 8
CTX = 32768
TOKENS = 512
DEVICES = 32


def draw_queries(key, part):
    shape_full = (TOKENS, HEADS, HEAD_DIM)
    base_draw = jnp.clip(jax.random.normal(jax.random.fold_in(key, 21), shape_full, jnp.float32), -8.0, 8.0)
    return base_draw.reshape(TOKENS, HEADS * HEAD_DIM).astype(jnp.bfloat16)


def draw_cache_keys(key, part):
    shape_full = (KV_HEADS, CTX, HEAD_DIM)
    drawn = jnp.clip(2.0 * jax.random.normal(jax.random.fold_in(key, 31), shape_full, jnp.float32), -8.0, 8.0)
    return drawn.astype(jnp.bfloat16)


def draw_block_lists(key, part):
    list_count = TOKENS // BLK * KV_HEADS
    per_device = CTX_DEV // BLK
    list_keys = jax.random.split(jax.random.fold_in(key, 41), list_count)

    def one_list(list_key):
        middle = jax.random.permutation(list_key, DEVICES - 2)[:NSEL - 2] + 1
        offsets = jax.random.randint(jax.random.fold_in(list_key, 1), (NSEL - 2,), 0, per_device)
        anchored = jnp.array([0, DEVICES * per_device - 1], dtype=jnp.int32)
        return jnp.concatenate([anchored, (middle * per_device + offsets).astype(jnp.int32)])
    return jax.vmap(one_list)(list_keys).reshape(TOKENS // BLK, KV_HEADS, NSEL)


def steps_of(own_key, extent, cuts, smallest, largest):
    def one(dim, shards_of):
        steps = jax.random.uniform(jax.random.fold_in(jax.random.fold_in(own_key, 6), dim), (shards_of,), jnp.float32, smallest / len(cuts), largest / len(cuts))
        return jnp.repeat(jnp.exp(steps), extent[dim] // shards_of).reshape((-1,) + (1,) * (len(extent) - dim - 1))

    gain = one(*cuts[0])
    for cut in cuts[1:]:
        gain = gain * one(*cut)
    return gain


def noise(key, dims, spread, most, pieces=(), kind=jnp.bfloat16):
    entries = jax.random.normal(key, dims, jnp.float32) * spread
    if len(pieces) > 0:
        entries = steps_of(key, dims, pieces, -0.22, 0.18) * entries
    return jnp.clip(entries, min=-most, max=most).astype(kind)


def setup_inputs(seed: int = 0) -> dict:
    keys = jax.random.split(jax.random.key(seed), 13)
    return {
        "queries": draw_queries(jax.random.fold_in(keys[12], 71), 0),
        "cache_keys": draw_cache_keys(jax.random.fold_in(keys[12], 71), 0),
        "cache_values": noise(keys[2], (KV_HEADS, CTX, HEAD_DIM), 1.0, 6.0, ((1, 32),)),
        "stretch_keys": noise(keys[3], (KV_HEADS, TOKENS, HEAD_DIM), 2.0, 8.0, ((1, 4),)),
        "stretch_values": noise(keys[4], (KV_HEADS, TOKENS, HEAD_DIM), 1.0, 6.0, ((1, 4),)),
        "block_lists": draw_block_lists(jax.random.fold_in(keys[12], 71), 0),
        "out_weight": noise(keys[6], (HEADS * HEAD_DIM, D), (HEADS * HEAD_DIM // 64) ** -0.5, 0.5, ((0, 8), (1, 4))),
        "residual": noise(keys[7], (TOKENS, D), 1.0, 6.0, ((0, 8), (1, 4))),
        "norm_gain": jnp.clip(1.0 + 0.15 * jax.random.normal(keys[8], (D,), jnp.float32), 0.25, 1.75).astype(jnp.bfloat16),
        "gate_weight": noise(keys[9], (D, FF), D ** -0.5, 0.0625, ((0, 4), (1, 8))),
        "up_weight": noise(keys[10], (D, FF), D ** -0.5, 0.0625, ((0, 4), (1, 8))),
        "down_weight": noise(keys[11], (FF, D), FF ** -0.5, 0.03125, ((0, 8), (1, 4))),
    }


def reference(queries, cache_keys, cache_values, stretch_keys, stretch_values, block_lists, out_weight, residual, norm_gain, gate_weight, up_weight, down_weight):
    scaling = 1.0 / math.sqrt(HEAD_DIM)
    query_blocks = TOKENS // BLK
    keys_blocked = cache_keys.reshape(KV_HEADS, CTX // BLK, BLK, HEAD_DIM)
    values_blocked = cache_values.reshape(KV_HEADS, CTX // BLK, BLK, HEAD_DIM)
    grouped = queries.reshape(query_blocks, BLK, KV_HEADS, GROUP, HEAD_DIM)
    row_pos = jnp.arange(BLK * GROUP, dtype=jnp.int32) // GROUP
    key_pos = jnp.arange(TOKENS, dtype=jnp.int32)

    def attend(item_index):
        block_index = item_index // KV_HEADS
        head_index = item_index % KV_HEADS
        query_rows = grouped[block_index, :, head_index].reshape(BLK * GROUP, HEAD_DIM)
        chosen = block_lists[block_index, head_index]
        far_keys = keys_blocked[head_index][chosen].reshape(NSEL * BLK, HEAD_DIM)
        far_values = values_blocked[head_index][chosen].reshape(NSEL * BLK, HEAD_DIM)
        near_keys = stretch_keys[head_index]
        near_values = stretch_values[head_index]
        far_scores = jnp.dot(query_rows, far_keys.T, preferred_element_type=jnp.float32) * scaling
        near_scores = jnp.dot(query_rows, near_keys.T, preferred_element_type=jnp.float32) * scaling
        allowed = key_pos[None, :] <= (block_index * BLK + row_pos)[:, None]
        near_scores = jnp.where(allowed, near_scores, -1e+30)
        row_top = jnp.maximum(lax.optimization_barrier(jnp.max(far_scores, axis=1)), lax.optimization_barrier(jnp.max(near_scores, axis=1)))
        far_exp = jnp.exp(far_scores - row_top[:, None])
        near_exp = jnp.where(allowed, jnp.exp(near_scores - row_top[:, None]), 0.0)
        totals = lax.optimization_barrier(jnp.sum(far_exp, axis=1)) + lax.optimization_barrier(jnp.sum(near_exp, axis=1))
        mixed_rows = jnp.dot(far_exp.astype(jnp.bfloat16), far_values, preferred_element_type=jnp.float32)
        mixed_rows = mixed_rows + jnp.dot(near_exp.astype(jnp.bfloat16), near_values, preferred_element_type=jnp.float32)
        return (mixed_rows / totals[:, None]).astype(jnp.bfloat16).reshape(BLK, GROUP * HEAD_DIM)
    outputs = lax.map(attend, jnp.arange(query_blocks * KV_HEADS, dtype=jnp.int32))
    outputs = outputs.reshape(query_blocks, KV_HEADS, BLK, GROUP * HEAD_DIM)
    attended = jnp.transpose(outputs, (0, 2, 1, 3)).reshape(TOKENS, HEADS * HEAD_DIM)
    stream = residual.astype(jnp.float32) + jnp.dot(attended, out_weight, preferred_element_type=jnp.float32)
    squares = lax.optimization_barrier(jnp.mean(stream * stream, axis=1))
    normed = (stream * lax.rsqrt(squares + 1e-05)[:, None] * norm_gain.astype(jnp.float32)).astype(jnp.bfloat16)
    gate_proj = jnp.dot(normed, gate_weight, preferred_element_type=jnp.float32)
    up_proj = jnp.dot(normed, up_weight, preferred_element_type=jnp.float32)
    hidden = (jax.nn.silu(gate_proj) * up_proj).astype(jnp.bfloat16)
    lowered = jnp.dot(hidden, down_weight, preferred_element_type=jnp.float32)
    return (stream + lowered).astype(jnp.bfloat16)
```

```python
import functools
import math

import jax
import jax.numpy as jnp
from jax import lax
from jax.experimental import pallas as pl
from jax.experimental.pallas import tpu as pltpu
from jax.sharding import PartitionSpec as P

KV_HEADS = 8
HEAD_DIM = 128
BLK = 128
GROUP = 8
SLOTS = 4
MESH = pl.DeviceIdType.MESH
NC = 4
STEPS = 7


def tail_kernel(
    cols,
    rows,
    att_ref,
    wo_ref,
    res_ref,
    gain_ref,
    gate_ref,
    up_ref,
    down_ref,
    out_ref,
    gate_buf,
    up_buf,
    down_buf,
    att_buf,
    part,
    first,
    mid,
    second,
    stream,
    square_own,
    square_buf,
    pieces,
    gate_part,
    up_part,
    gate_first,
    up_first,
    gate_mid,
    up_mid,
    gate_second,
    up_second,
    left,
    right,
    total,
    gate_sem,
    up_sem,
    down_sem,
    wo_sem,
    att_send,
    att_recv,
    rs_pair_send,
    rs_pair_recv,
    rs_line_send,
    rs_line_recv,
    square_send,
    square_recv,
    ag_line_send,
    ag_line_recv,
    ag_pair_send,
    ag_pair_recv,
    pair_send,
    pair_recv,
    line_send,
    line_recv,
):
    col = lax.axis_index("col")
    row = lax.axis_index("row")
    steps = gate_buf.shape[0]
    wide = gate_buf.shape[2]
    half = wide // 2
    share = gate_part.shape[3]
    _, toks, width = out_ref.shape
    many = cols * share
    spare = wo_ref.shape[0] // wide
    tile = min(512, width)
    col_lines = cols // 2
    pair_me = lax.rem(col, 2)
    line_me = col // 2
    col_other = line_me * 2 + (1 - pair_me)
    row_lines = rows // 2
    core = lax.rem(row, 2)
    depth_me = row // 2
    row_other = depth_me * 2 + (1 - core)

    def line(k):
        return lax.rem(line_me + k, col_lines)

    def layer(k):
        return lax.rem(depth_me + k, row_lines)

    def remote(src, dst, send, recv, axis, device):
        return pltpu.make_async_remote_copy(
            src_ref=src,
            dst_ref=dst,
            send_sem=send,
            recv_sem=recv,
            device_id={axis: device},
            device_id_type=MESH,
        )

    def gate_copy(j):
        return pltpu.make_async_copy(
            gate_ref.at[:, pl.ds(pl.multiple_of(j * wide, wide), wide)], gate_buf.at[j], gate_sem.at[j]
        )

    def up_copy(j):
        return pltpu.make_async_copy(
            up_ref.at[:, pl.ds(pl.multiple_of(j * wide, wide), wide)], up_buf.at[j], up_sem.at[j]
        )

    def down_copy(j):
        return pltpu.make_async_copy(
            down_ref.at[pl.ds(pl.multiple_of(j * wide, wide), wide), :], down_buf.at[j], down_sem.at[j]
        )

    def wo_copy(p):
        return pltpu.make_async_copy(
            wo_ref.at[p * wide : (p + 1) * wide, :], down_buf.at[steps - spare + p], wo_sem.at[p]
        )

    def att_copy(q, k):
        return remote(
            att_ref.at[:, q * toks : (q + 1) * toks, :],
            att_buf.at[q, col],
            att_send.at[q, k - 1],
            att_recv.at[q, k - 1],
            "col",
            lax.rem(col + k, cols),
        )

    def rs_pair(w, q):
        return remote(
            part.at[w, q, :, 1 - core],
            first.at[w, q],
            rs_pair_send.at[w, q],
            rs_pair_recv.at[w, q],
            "row",
            row_other,
        )

    def rs_line(w, q, k):
        return remote(
            mid.at[w, q, layer(k)],
            second.at[w, q, k - 1],
            rs_line_send.at[w, q, k - 1],
            rs_line_recv.at[w, q, k - 1],
            "row",
            layer(k) * 2 + core,
        )

    def rs_middle(w, q):
        rs_pair(w, q).wait()
        for d in range(row_lines):
            mid[w, q, d] = (
                part[w, q, d, core].astype(jnp.float32) + first[w, q, d].astype(jnp.float32)
            ).astype(jnp.bfloat16)

    def rs_lines_start(w, q):
        for k in range(1, row_lines):
            rs_line(w, q, k).start()

    def rs_finish(w, q):
        result = mid[w, q, depth_me].astype(jnp.float32)
        for k in range(1, row_lines):
            rs_line(w, q, k).wait()
            result = result + second[w, q, k - 1].astype(jnp.float32)
        return result

    def square_copy(q, k):
        return remote(
            square_own.at[q],
            square_buf.at[q, k - 1],
            square_send.at[q, k - 1],
            square_recv.at[q, k - 1],
            "col",
            lax.rem(col + k, cols),
        )

    def stream_step(q):
        value = rs_finish(0, q) + res_ref[q].astype(jnp.float32)
        stream[q] = value
        squares = jnp.sum(value * value, axis=1, keepdims=True)
        square_own[q] = jnp.broadcast_to(squares, (toks, 128))
        for k in range(1, cols):
            square_copy(q, k).start()

    def ag_line(q, k):
        return remote(
            pieces.at[q, depth_me, core],
            pieces.at[q, depth_me, core],
            ag_line_send.at[q, k - 1],
            ag_line_recv.at[q, k - 1],
            "row",
            layer(k) * 2 + core,
        )

    def ag_pair(q, k):
        owner = layer(row_lines - k)
        return remote(
            pieces.at[q, owner, core],
            pieces.at[q, owner, core],
            ag_pair_send.at[q, k],
            ag_pair_recv.at[q, k],
            "row",
            row_other,
        )

    def norm_step(q):
        squares = square_own[q]
        for k in range(1, cols):
            square_copy(q, k).wait()
            squares = squares + square_buf[q, k - 1]
        factor = lax.rsqrt(squares / (width * cols) + 1e-05)[:, :1]
        pieces[q, depth_me, core] = (stream[q] * factor * gain_ref[...].astype(jnp.float32)).astype(
            jnp.bfloat16
        )
        for k in range(1, row_lines):
            ag_line(q, k).start()
        ag_pair(q, 0).start()

    def ag_forward(q):
        for k in range(1, row_lines):
            ag_line(q, k).wait()
            ag_pair(q, k).start()

    def ag_done(q):
        for k in range(row_lines):
            ag_pair(q, k).wait()

    def transfers(stage, slot):
        if stage == 0:
            pair = (gate_part.at[slot, 1 - pair_me], gate_first.at[slot])
            along = [(up_part.at[slot, line(k)], up_first.at[slot, k - 1]) for k in range(1, col_lines)]
        elif stage == 1:
            pair = (up_mid.at[slot, 1 - pair_me], up_second.at[slot])
            along = [(gate_mid.at[slot, line(k)], gate_second.at[slot, k - 1]) for k in range(1, col_lines)]
        elif stage == 2:
            pair = (left.at[slot, 0, 0], left.at[slot, 0, 1])
            along = [(right.at[slot, 0, 0], right.at[slot, 0, k]) for k in range(1, col_lines)]
        else:
            pair = (right.at[slot, 0], right.at[slot, 1])
            along = [(left.at[slot, 0], left.at[slot, k]) for k in range(1, col_lines)]
        copies = [
            remote(*pair, pair_send.at[stage, slot], pair_recv.at[stage, slot], "col", col_other)
        ]
        for k in range(1, col_lines):
            copies.append(
                remote(
                    *along[k - 1],
                    line_send.at[stage, slot, k - 1],
                    line_recv.at[stage, slot, k - 1],
                    "col",
                    line(k) * 2 + pair_me,
                )
            )
        return copies

    for p in range(spare):
        wo_copy(p).start()
    for j in range(steps):
        gate_copy(j).start()
        up_copy(j).start()
        if j < steps - spare:
            down_copy(j).start()
    barrier = pltpu.get_barrier_semaphore()
    for k in range(1, cols):
        pl.semaphore_signal(
            barrier, inc=1, device_id={"col": lax.rem(col + k, cols)}, device_id_type=MESH
        )
    pl.semaphore_signal(barrier, inc=1, device_id={"row": row_other}, device_id_type=MESH)
    for k in range(1, row_lines):
        pl.semaphore_signal(
            barrier, inc=1, device_id={"row": layer(k) * 2 + core}, device_id_type=MESH
        )
    pl.semaphore_wait(barrier, cols - 1 + row_lines)
    for q in range(NC):
        for k in range(1, cols):
            att_copy(q, k).start()
    total[...] = jnp.zeros_like(total)
    for p in range(spare):
        wo_copy(p).wait()

    for q in range(NC):
        att_buf[q, col] = att_ref[:, q * toks : (q + 1) * toks, :]
        for k in range(1, cols):
            att_copy(q, k).wait()
        inputs = att_buf[q].reshape(many, att_buf.shape[-1])
        for start in range(0, width, tile):
            product = jnp.zeros((many, tile), jnp.float32)
            for p in range(spare):
                product = product + jnp.dot(
                    inputs[:, p * wide : (p + 1) * wide],
                    down_buf[steps - spare + p, :, start : start + tile],
                    preferred_element_type=jnp.float32,
                )
            part[0, q, :, :, :, start : start + tile] = product.astype(jnp.bfloat16).reshape(
                row_lines, 2, toks, tile
            )
        rs_pair(0, q).start()
        rs_middle(0, q)
        if q == 0:
            rs_lines_start(0, 0)
    for j in range(steps - spare, steps):
        down_copy(j).start()
    stream_step(0)
    norm_step(0)
    if NC > 1:
        rs_lines_start(0, 1)
    ag_forward(0)

    chunks = NC * steps

    def stage_when(i, stage):
        return pl.when((i >= stage) & (i < chunks + stage))

    def iteration(i, carry):
        q_now = i // steps
        j_now = lax.rem(i, steps)

        @pl.when((j_now == 0) & (q_now < NC))
        def _():
            ag_done(q_now)

        @stage_when(i, 0)
        def _():
            @pl.when(i < steps)
            def _():
                gate_copy(i).wait()
                up_copy(i).wait()

            slot = lax.rem(i, SLOTS)
            inputs = pieces[q_now].reshape(many, pieces.shape[-1])
            product = jnp.dot(inputs, gate_buf[j_now], preferred_element_type=jnp.float32).astype(jnp.bfloat16)
            for b in range(cols):
                gate_part[slot, b % 2, b // 2] = product[b * share : (b + 1) * share]
            product = jnp.dot(inputs, up_buf[j_now], preferred_element_type=jnp.float32).astype(jnp.bfloat16)
            for b in range(cols):
                up_part[slot, b // 2, b % 2] = product[b * share : (b + 1) * share]
            for copy in transfers(0, slot):
                copy.start()

        @stage_when(i, 1)
        def _():
            slot = lax.rem(i - 1, SLOTS)
            for copy in transfers(0, slot):
                copy.wait()
            gate_mid[slot] = (
                gate_part[slot, pair_me].astype(jnp.float32) + gate_first[slot].astype(jnp.float32)
            ).astype(jnp.bfloat16)
            up_sum = up_part[slot, line_me].astype(jnp.float32)
            for k in range(1, col_lines):
                up_sum = up_sum + up_first[slot, k - 1].astype(jnp.float32)
            up_mid[slot] = up_sum.astype(jnp.bfloat16)
            for copy in transfers(1, slot):
                copy.start()

        @stage_when(i, 2)
        def _():
            slot = lax.rem(i - 2, SLOTS)
            for copy in transfers(1, slot):
                copy.wait()
            gate = gate_mid[slot, line_me].astype(jnp.float32)
            for k in range(1, col_lines):
                gate = gate + gate_second[slot, k - 1].astype(jnp.float32)
            up = up_mid[slot, pair_me].astype(jnp.float32) + up_second[slot].astype(jnp.float32)
            hidden = (gate / (1.0 + jnp.exp(-gate)) * up).astype(jnp.bfloat16)
            left[slot, 0, 0] = hidden[:, :half]
            right[slot, 0, 0] = hidden[:, half:]
            for copy in transfers(2, slot):
                copy.start()

        @stage_when(i, 3)
        def _():
            slot = lax.rem(i - 3, SLOTS)
            for copy in transfers(2, slot):
                copy.wait()
            for copy in transfers(3, slot):
                copy.start()

        @stage_when(i, 4)
        def _():
            j = lax.rem(i - 4, steps)
            slot = lax.rem(i - 4, SLOTS)

            @pl.when(i - 4 < steps)
            def _():
                down_copy(i - 4).wait()

            for copy in transfers(3, slot):
                copy.wait()
            gathered = jnp.concatenate(
                [
                    jnp.concatenate([left[slot, k, p], right[slot, p, k]], axis=1)
                    for p in range(2)
                    for k in range(col_lines)
                ],
                axis=0,
            )
            for start in range(0, width, tile):
                total[:, start : start + tile] += jnp.dot(
                    gathered,
                    down_buf[j, :, start : start + tile],
                    preferred_element_type=jnp.float32,
                )

        @pl.when((j_now == 1) & (q_now + 1 < NC))
        def _():
            stream_step(q_now + 1)

        @pl.when((j_now == 2) & (q_now + 1 < NC))
        def _():
            norm_step(q_now + 1)

        @pl.when((j_now == 2) & (q_now + 2 < NC))
        def _():
            rs_lines_start(0, q_now + 2)

        @pl.when((j_now == 5) & (q_now + 1 < NC))
        def _():
            ag_forward(q_now + 1)

        @pl.when((i >= steps + 3) & (lax.rem(i - 3, steps) == 0))
        def _():
            q = (i - 4) // steps
            for p in range(2):
                for k in range(col_lines):
                    owner = line(col_lines - k) * 2 + lax.rem(pair_me + p, 2)
                    begin = (p * col_lines + k) * share
                    part[1, q, owner] = (
                        total[begin : begin + share, :].astype(jnp.bfloat16).reshape(2, toks, width)
                    )
            rs_pair(1, q).start()
            total[...] = jnp.zeros_like(total)

        @pl.when((i >= steps + 4) & (lax.rem(i - 4, steps) == 0))
        def _():
            q = (i - 5) // steps
            rs_middle(1, q)
            rs_lines_start(1, q)

        @pl.when((i >= steps + 8) & (lax.rem(i - 8, steps) == 0))
        def _():
            q = (i - 9) // steps
            out_ref[q] = (stream[q] + rs_finish(1, q)).astype(jnp.bfloat16)

        return carry

    lax.fori_loop(0, chunks + 4, iteration, 0)
    rs_middle(1, NC - 1)
    rs_lines_start(1, NC - 1)
    out_ref[NC - 1] = (stream[NC - 1] + rs_finish(1, NC - 1)).astype(jnp.bfloat16)


def tail(attended, out_weight, residual, norm_gain, gate_weight, up_weight, down_weight):
    cols = lax.axis_size("col")
    rows = lax.axis_size("row")
    depth, hidden_width = gate_weight.shape
    tokens, width = residual.shape
    inner = out_weight.shape[0]
    wide = hidden_width // STEPS
    toks = tokens // NC
    share = rows * toks // cols
    col_lines = cols // 2
    row_lines = rows // 2
    assert rows == 2 * cols and inner % wide == 0
    vmem = pl.BlockSpec(memory_space=pltpu.VMEM)
    hbm = pl.BlockSpec(memory_space=pl.ANY)
    dma = pltpu.SemaphoreType.DMA

    def held(*shape):
        return pltpu.VMEM(shape, jnp.bfloat16)

    out = pl.pallas_call(
        functools.partial(tail_kernel, cols, rows),
        out_shape=jax.ShapeDtypeStruct((NC, toks, width), jnp.bfloat16),
        in_specs=[vmem, hbm, vmem, vmem, hbm, hbm, hbm],
        out_specs=vmem,
        scratch_shapes=[
            held(STEPS, depth, wide),
            held(STEPS, depth, wide),
            held(STEPS, wide, width),
            held(NC, cols, 2, toks, inner),
            held(2, NC, row_lines, 2, toks, width),
            held(2, NC, row_lines, toks, width),
            held(2, NC, row_lines, toks, width),
            held(2, NC, row_lines - 1, toks, width),
            pltpu.VMEM((NC, toks, width), jnp.float32),
            pltpu.VMEM((NC, toks, 128), jnp.float32),
            pltpu.VMEM((NC, cols - 1, toks, 128), jnp.float32),
            held(NC, row_lines, 2, toks, depth),
            held(SLOTS, 2, col_lines, share, wide),
            held(SLOTS, col_lines, 2, share, wide),
            held(SLOTS, col_lines, share, wide),
            held(SLOTS, col_lines - 1, 2, share, wide),
            held(SLOTS, col_lines, share, wide),
            held(SLOTS, 2, share, wide),
            held(SLOTS, col_lines - 1, share, wide),
            held(SLOTS, share, wide),
            held(SLOTS, col_lines, 2, share, wide // 2),
            held(SLOTS, 2, col_lines, share, wide // 2),
            pltpu.VMEM((cols * share, width), jnp.float32),
            dma((STEPS,)),
            dma((STEPS,)),
            dma((STEPS,)),
            dma((inner // wide,)),
            dma((NC, cols - 1)),
            dma((NC, cols - 1)),
            dma((2, NC)),
            dma((2, NC)),
            dma((2, NC, row_lines - 1)),
            dma((2, NC, row_lines - 1)),
            dma((NC, cols - 1)),
            dma((NC, cols - 1)),
            dma((NC, row_lines - 1)),
            dma((NC, row_lines - 1)),
            dma((NC, row_lines)),
            dma((NC, row_lines)),
            dma((4, SLOTS)),
            dma((4, SLOTS)),
            dma((4, SLOTS, col_lines - 1)),
            dma((4, SLOTS, col_lines - 1)),
        ],
        compiler_params=pltpu.CompilerParams(
            collective_id=0, has_side_effects=True, vmem_limit_bytes=66 * 1000 * 1000
        ),
    )(
        attended.reshape(2, tokens, inner),
        out_weight,
        residual.reshape(NC, toks, width),
        norm_gain.reshape(1, width),
        gate_weight,
        up_weight,
        down_weight,
    )
    return out.reshape(tokens, width)


def local(
    queries,
    cache_keys,
    cache_values,
    stretch_keys,
    stretch_values,
    block_lists,
    out_weight,
    residual,
    norm_gain,
    gate_weight,
    up_weight,
    down_weight,
):
    row_count = lax.axis_size("row")
    col_count = lax.axis_size("col")
    row_index = lax.axis_index("row")
    col_index = lax.axis_index("col")
    device_count = row_count * col_count
    my_index = row_index * col_count + col_index
    local_blocks = cache_keys.shape[1] // BLK
    heads_here = queries.shape[1] // HEAD_DIM
    list_length = block_lists.shape[2]
    my_group = row_index * heads_here // GROUP
    scaling = 1.0 / math.sqrt(HEAD_DIM)
    targets = jnp.arange(device_count, dtype=jnp.int32)
    target_group = targets // col_count * heads_here // GROUP
    target_lists = block_lists[targets % col_count, target_group]
    holders = target_lists // local_blocks
    matched = holders == my_index
    found_any = jnp.any(matched, axis=1)
    within = jnp.sum(jnp.where(matched, target_lists % local_blocks, 0), axis=1)
    source_rows = target_group * local_blocks + within
    flat_keys = cache_keys.reshape(KV_HEADS * local_blocks, BLK, HEAD_DIM)
    flat_values = cache_values.reshape(KV_HEADS * local_blocks, BLK, HEAD_DIM)
    outgoing = jnp.concatenate([flat_keys[source_rows], flat_values[source_rows]], axis=2)
    outgoing = jnp.where(found_any[:, None, None], outgoing, jnp.zeros_like(outgoing))
    arrived = lax.all_to_all(outgoing, ("row", "col"), split_axis=0, concat_axis=0, tiled=True)
    my_list = block_lists[col_index, my_group]
    fetched = arrived[my_list // local_blocks].reshape(list_length * BLK, 2 * HEAD_DIM)
    far_keys = fetched[:, :HEAD_DIM]
    far_values = fetched[:, HEAD_DIM:]
    query_rows = queries.reshape(BLK * heads_here, HEAD_DIM)
    far_scores = jnp.dot(query_rows, far_keys.T, preferred_element_type=jnp.float32) * scaling
    run_max = jnp.max(far_scores, axis=1)
    far_exp = jnp.exp(far_scores - run_max[:, None])
    run_sum = jnp.sum(far_exp, axis=1)
    run_acc = jnp.dot(far_exp.astype(jnp.bfloat16), far_values, preferred_element_type=jnp.float32)
    query_pos = col_index * BLK + jnp.arange(BLK * heads_here, dtype=jnp.int32) // heads_here
    own = jnp.concatenate([stretch_keys, stretch_values], axis=2)
    own = lax.dynamic_index_in_dim(own, my_group, 0, keepdims=False)
    piece = lax.all_gather(own, "col", axis=0, tiled=True)
    piece_keys = piece[:, :HEAD_DIM]
    piece_values = piece[:, HEAD_DIM:]
    scores = jnp.dot(query_rows, piece_keys.T, preferred_element_type=jnp.float32) * scaling
    key_pos = jnp.arange(piece_keys.shape[0], dtype=jnp.int32)
    allowed = key_pos[None, :] <= query_pos[:, None]
    scores = jnp.where(allowed, scores, -1e30)
    new_max = jnp.maximum(run_max, jnp.max(scores, axis=1))
    decays = jnp.exp(run_max - new_max)
    weights = jnp.where(allowed, jnp.exp(scores - new_max[:, None]), 0.0)
    new_sum = run_sum * decays + jnp.sum(weights, axis=1)
    new_acc = run_acc * decays[:, None] + jnp.dot(
        weights.astype(jnp.bfloat16), piece_values, preferred_element_type=jnp.float32
    )
    attended = (new_acc / new_sum[:, None]).astype(jnp.bfloat16).reshape(BLK, heads_here * HEAD_DIM)
    return tail(attended, out_weight, residual, norm_gain, gate_weight, up_weight, down_weight)


def solution(mesh):
    in_specs = (
        P("col", "row"),
        P(None, ("row", "col"), None),
        P(None, ("row", "col"), None),
        P(None, "col", None),
        P(None, "col", None),
        P(),
        P("row", "col"),
        P("row", "col"),
        P("col"),
        P("col", "row"),
        P("col", "row"),
        P("row", "col"),
    )
    out_specs = P("row", "col")
    return jax.shard_map(local, mesh=mesh, in_specs=in_specs, out_specs=out_specs, check_vma=False)
```

```python
import functools
import math

import jax
import jax.numpy as jnp
from jax import lax
from jax.experimental import pallas as pl
from jax.experimental.pallas import tpu as pltpu
from jax.sharding import PartitionSpec as P

KV_HEADS = 8
HEAD_DIM = 128
BLK = 128
GROUP = 8
SLOTS = 4
MESH = pl.DeviceIdType.MESH
NC = 4
STEPS = 7


def gather_kernel(devices, rows_ref, keys_ref, values_ref, out_ref, key_sem, value_sem):
    groups = keys_ref.shape[0]

    def copies(d):
        group = d * groups // devices
        positions = pl.ds(pl.multiple_of(rows_ref[d] * BLK, BLK), BLK)
        return (
            pltpu.make_async_copy(keys_ref.at[group, positions], out_ref.at[d, 0], key_sem.at[d]),
            pltpu.make_async_copy(values_ref.at[group, positions], out_ref.at[d, 1], value_sem.at[d]),
        )

    for d in range(devices):
        for copy in copies(d):
            copy.start()
    for d in range(devices):
        for copy in copies(d):
            copy.wait()


def gather_blocks(block_rows, cache_keys, cache_values):
    devices = block_rows.shape[0]
    dma = pltpu.SemaphoreType.DMA
    return pl.pallas_call(
        functools.partial(gather_kernel, devices),
        out_shape=jax.ShapeDtypeStruct((devices, 2, BLK, HEAD_DIM), cache_keys.dtype),
        in_specs=[
            pl.BlockSpec(memory_space=pltpu.SMEM),
            pl.BlockSpec(memory_space=pl.ANY),
            pl.BlockSpec(memory_space=pl.ANY),
        ],
        out_specs=pl.BlockSpec(memory_space=pltpu.VMEM),
        scratch_shapes=[dma((devices,)), dma((devices,))],
        compiler_params=pltpu.CompilerParams(vmem_limit_bytes=16 * 1024 * 1024),
    )(block_rows, cache_keys, cache_values)


def flipped(index, bits):
    result = index
    place = 1
    while place <= bits:
        if bits // place % 2:
            result = result + place * (1 - 2 * lax.rem(index // place, 2))
        place *= 2
    return result


def attend_kernel(
    rows,
    cols,
    query_ref,
    block_ref,
    bias_ref,
    near_key_ref,
    near_value_ref,
    out_ref,
    held,
    near,
    heads_first,
    top,
    norm,
    acc,
    near_sem,
    near_send,
    near_recv,
    block_send,
    block_recv,
):
    row = lax.axis_index("row")
    col = lax.axis_index("col")
    devices = rows * cols
    heads = query_ref.shape[1] // HEAD_DIM
    group = row * heads // GROUP
    scaling = 1.0 / math.sqrt(HEAD_DIM)
    pairs = heads // 2
    order = sorted(range(devices), key=lambda k: (k // cols // 2, k))
    slot_of = {k: s for s, k in enumerate(order)}

    def peer(k):
        return flipped(row, k // cols), flipped(col, k % cols)

    def block_copy(k):
        peer_row, peer_col = peer(k)
        slot = slot_of[k]
        return pltpu.make_async_remote_copy(
            src_ref=block_ref.at[peer_row * cols + peer_col],
            dst_ref=held.at[slot],
            send_sem=block_send.at[slot],
            recv_sem=block_recv.at[slot],
            device_id={"row": peer_row, "col": peer_col},
            device_id_type=MESH,
        )

    def near_copy(k):
        return pltpu.make_async_remote_copy(
            src_ref=near.at[col],
            dst_ref=near.at[col],
            send_sem=near_send.at[k - 1],
            recv_sem=near_recv.at[k - 1],
            device_id={"col": flipped(col, k)},
            device_id_type=MESH,
        )

    own = (
        pltpu.make_async_copy(near_key_ref.at[group], near.at[col, 0], near_sem.at[0]),
        pltpu.make_async_copy(near_value_ref.at[group], near.at[col, 1], near_sem.at[1]),
    )
    for copy in own:
        copy.start()
    barrier = pltpu.get_barrier_semaphore()
    for k in range(1, devices):
        peer_row, peer_col = peer(k)
        pl.semaphore_signal(
            barrier, inc=1, device_id={"row": peer_row, "col": peer_col}, device_id_type=MESH
        )
    pl.semaphore_wait(barrier, devices - 1)
    for copy in own:
        copy.wait()
    for k in range(1, cols):
        near_copy(k).start()
    for k in sorted(range(1, devices), key=lambda k: (-(k // cols // 2), k)):
        block_copy(k).start()
    held[0] = block_ref[row * cols + col]
    for h in range(heads):
        heads_first[h * BLK : (h + 1) * BLK, :] = query_ref[:, h * HEAD_DIM : (h + 1) * HEAD_DIM]
    for k in range(1, cols):
        near_copy(k).wait()

    def near_pass(p, carry):
        lines = pl.ds(pl.multiple_of(p * 2 * BLK, 2 * BLK), 2 * BLK)
        keys = near[:, 0].reshape(cols * BLK, HEAD_DIM)
        scores = lax.dot_general(
            heads_first[lines, :], keys, (((1,), (1,)), ((), ())), preferred_element_type=jnp.float32
        ) * scaling
        position = lax.broadcasted_iota(jnp.int32, scores.shape, 1)
        token = col * BLK + lax.rem(lax.broadcasted_iota(jnp.int32, scores.shape, 0), BLK)
        allowed = position <= token
        scores = jnp.where(allowed, scores, -1e30)
        new_top = jnp.max(scores, axis=1, keepdims=True)
        weights = jnp.where(allowed, jnp.exp(scores - new_top), 0.0)
        top[lines, :] = jnp.broadcast_to(new_top, (2 * BLK, HEAD_DIM))
        norm[lines, :] = jnp.broadcast_to(jnp.sum(weights, axis=1, keepdims=True), (2 * BLK, HEAD_DIM))
        acc[lines, :] = jnp.dot(
            weights.astype(jnp.bfloat16),
            near[:, 1].reshape(cols * BLK, HEAD_DIM),
            preferred_element_type=jnp.float32,
        )
        return carry

    lax.fori_loop(0, pairs, near_pass, 0)

    batch = 4
    for first in range(0, devices, batch):
        bias = []
        for slot in range(first, first + batch):
            k = order[slot]
            if k:
                block_copy(k).wait()
            peer_row, peer_col = peer(k)
            bias.append(bias_ref[peer_row * cols + peer_col])
        bias = jnp.concatenate(bias, axis=1)

        def far_pass(p, carry):
            lines = pl.ds(pl.multiple_of(p * 2 * BLK, 2 * BLK), 2 * BLK)
            keys = held[first : first + batch, 0].reshape(batch * BLK, HEAD_DIM)
            scores = (
                lax.dot_general(
                    heads_first[lines, :], keys, (((1,), (1,)), ((), ())), preferred_element_type=jnp.float32
                )
                * scaling
                + bias
            )
            old_top = top[lines, :]
            new_top = jnp.maximum(old_top, jnp.max(scores, axis=1, keepdims=True))
            decay = jnp.exp(old_top - new_top)
            weights = jnp.exp(scores - new_top[:, :1])
            top[lines, :] = new_top
            norm[lines, :] = norm[lines, :] * decay + jnp.sum(weights, axis=1, keepdims=True)
            acc[lines, :] = acc[lines, :] * decay + jnp.dot(
                weights.astype(jnp.bfloat16),
                held[first : first + batch, 1].reshape(batch * BLK, HEAD_DIM),
                preferred_element_type=jnp.float32,
            )
            return carry

        lax.fori_loop(0, pairs, far_pass, 0)
    halves = out_ref.shape[1]
    for h in range(heads):
        lines = slice(h * BLK, (h + 1) * BLK)
        result = (acc[lines, :] / norm[lines, :]).astype(jnp.bfloat16)
        for p in range(BLK // halves):
            out_ref[p, :, h * HEAD_DIM : (h + 1) * HEAD_DIM] = result[p * halves : (p + 1) * halves]


def attend(queries, blocks, bias, stretch_keys, stretch_values, tokens):
    rows = lax.axis_size("row")
    cols = lax.axis_size("col")
    devices = rows * cols
    lines = BLK * queries.shape[1] // HEAD_DIM
    vmem = pl.BlockSpec(memory_space=pltpu.VMEM)
    hbm = pl.BlockSpec(memory_space=pl.ANY)
    dma = pltpu.SemaphoreType.DMA
    return pl.pallas_call(
        functools.partial(attend_kernel, rows, cols),
        out_shape=jax.ShapeDtypeStruct((BLK // tokens, tokens, queries.shape[1]), jnp.bfloat16),
        in_specs=[vmem, vmem, vmem, hbm, hbm],
        out_specs=vmem,
        scratch_shapes=[
            pltpu.VMEM((devices, 2, BLK, HEAD_DIM), jnp.bfloat16),
            pltpu.VMEM((cols, 2, BLK, HEAD_DIM), jnp.bfloat16),
            pltpu.VMEM((lines, HEAD_DIM), jnp.bfloat16),
            pltpu.VMEM((lines, HEAD_DIM), jnp.float32),
            pltpu.VMEM((lines, HEAD_DIM), jnp.float32),
            pltpu.VMEM((lines, HEAD_DIM), jnp.float32),
            dma((2,)),
            dma((cols - 1,)),
            dma((cols - 1,)),
            dma((devices,)),
            dma((devices,)),
        ],
        compiler_params=pltpu.CompilerParams(
            collective_id=1, has_side_effects=True, vmem_limit_bytes=40 * 1024 * 1024
        ),
    )(queries, blocks, bias, stretch_keys, stretch_values)


def tail_kernel(
    cols,
    rows,
    att_ref,
    wo_ref,
    res_ref,
    gain_ref,
    gate_ref,
    up_ref,
    down_ref,
    out_ref,
    gate_buf,
    up_buf,
    down_buf,
    att_buf,
    part,
    first,
    mid,
    second,
    stream,
    square_own,
    square_buf,
    pieces,
    gate_part,
    up_part,
    gate_first,
    up_first,
    gate_mid,
    up_mid,
    gate_second,
    up_second,
    left,
    right,
    total,
    gate_sem,
    up_sem,
    down_sem,
    wo_sem,
    att_send,
    att_recv,
    rs_pair_send,
    rs_pair_recv,
    rs_line_send,
    rs_line_recv,
    square_send,
    square_recv,
    ag_line_send,
    ag_line_recv,
    ag_pair_send,
    ag_pair_recv,
    pair_send,
    pair_recv,
    line_send,
    line_recv,
):
    col = lax.axis_index("col")
    row = lax.axis_index("row")
    steps = gate_buf.shape[0]
    wide = gate_buf.shape[2]
    half = wide // 2
    share = gate_part.shape[3]
    _, toks, width = out_ref.shape
    many = cols * share
    spare = wo_ref.shape[0] // wide
    tile = min(512, width)
    col_lines = cols // 2
    pair_me = lax.rem(col, 2)
    line_me = col // 2
    col_other = line_me * 2 + (1 - pair_me)
    row_lines = rows // 2
    core = lax.rem(row, 2)
    depth_me = row // 2
    row_other = depth_me * 2 + (1 - core)

    def line(k):
        return lax.rem(line_me + k, col_lines)

    def layer(k):
        return lax.rem(depth_me + k, row_lines)

    def remote(src, dst, send, recv, axis, device):
        return pltpu.make_async_remote_copy(
            src_ref=src,
            dst_ref=dst,
            send_sem=send,
            recv_sem=recv,
            device_id={axis: device},
            device_id_type=MESH,
        )

    def gate_copy(j):
        return pltpu.make_async_copy(
            gate_ref.at[:, pl.ds(pl.multiple_of(j * wide, wide), wide)], gate_buf.at[j], gate_sem.at[j]
        )

    def up_copy(j):
        return pltpu.make_async_copy(
            up_ref.at[:, pl.ds(pl.multiple_of(j * wide, wide), wide)], up_buf.at[j], up_sem.at[j]
        )

    def down_copy(j):
        return pltpu.make_async_copy(
            down_ref.at[pl.ds(pl.multiple_of(j * wide, wide), wide), :], down_buf.at[j], down_sem.at[j]
        )

    def wo_copy(p):
        return pltpu.make_async_copy(
            wo_ref.at[p * wide : (p + 1) * wide, :], down_buf.at[steps - spare + p], wo_sem.at[p]
        )

    def att_copy(q, k):
        return remote(
            att_ref.at[:, q * toks : (q + 1) * toks, :],
            att_buf.at[q, col],
            att_send.at[q, k - 1],
            att_recv.at[q, k - 1],
            "col",
            lax.rem(col + k, cols),
        )

    def rs_pair(w, q):
        return remote(
            part.at[w, q, :, 1 - core],
            first.at[w, q],
            rs_pair_send.at[w, q],
            rs_pair_recv.at[w, q],
            "row",
            row_other,
        )

    def rs_line(w, q, k):
        return remote(
            mid.at[w, q, layer(k)],
            second.at[w, q, k - 1],
            rs_line_send.at[w, q, k - 1],
            rs_line_recv.at[w, q, k - 1],
            "row",
            layer(k) * 2 + core,
        )

    def rs_middle(w, q):
        rs_pair(w, q).wait()
        for d in range(row_lines):
            mid[w, q, d] = (
                part[w, q, d, core].astype(jnp.float32) + first[w, q, d].astype(jnp.float32)
            ).astype(jnp.bfloat16)

    def rs_lines_start(w, q):
        for k in range(1, row_lines):
            rs_line(w, q, k).start()

    def rs_finish(w, q):
        result = mid[w, q, depth_me].astype(jnp.float32)
        for k in range(1, row_lines):
            rs_line(w, q, k).wait()
            result = result + second[w, q, k - 1].astype(jnp.float32)
        return result

    def square_copy(q, k):
        return remote(
            square_own.at[q],
            square_buf.at[q, k - 1],
            square_send.at[q, k - 1],
            square_recv.at[q, k - 1],
            "col",
            lax.rem(col + k, cols),
        )

    def stream_step(q):
        value = rs_finish(0, q) + res_ref[q].astype(jnp.float32)
        stream[q] = value
        squares = jnp.sum(value * value, axis=1, keepdims=True)
        square_own[q] = jnp.broadcast_to(squares, (toks, 128))
        for k in range(1, cols):
            square_copy(q, k).start()

    def ag_line(q, k):
        return remote(
            pieces.at[q, depth_me, core],
            pieces.at[q, depth_me, core],
            ag_line_send.at[q, k - 1],
            ag_line_recv.at[q, k - 1],
            "row",
            layer(k) * 2 + core,
        )

    def ag_pair(q, k):
        owner = layer(row_lines - k)
        return remote(
            pieces.at[q, owner, core],
            pieces.at[q, owner, core],
            ag_pair_send.at[q, k],
            ag_pair_recv.at[q, k],
            "row",
            row_other,
        )

    def norm_step(q):
        squares = square_own[q]
        for k in range(1, cols):
            square_copy(q, k).wait()
            squares = squares + square_buf[q, k - 1]
        factor = lax.rsqrt(squares / (width * cols) + 1e-05)[:, :1]
        pieces[q, depth_me, core] = (stream[q] * factor * gain_ref[...].astype(jnp.float32)).astype(
            jnp.bfloat16
        )
        for k in range(1, row_lines):
            ag_line(q, k).start()
        ag_pair(q, 0).start()

    def ag_forward(q):
        for k in range(1, row_lines):
            ag_line(q, k).wait()
            ag_pair(q, k).start()

    def ag_done(q):
        for k in range(row_lines):
            ag_pair(q, k).wait()

    def transfers(stage, slot):
        if stage == 0:
            pair = (gate_part.at[slot, 1 - pair_me], gate_first.at[slot])
            along = [(up_part.at[slot, line(k)], up_first.at[slot, k - 1]) for k in range(1, col_lines)]
        elif stage == 1:
            pair = (up_mid.at[slot, 1 - pair_me], up_second.at[slot])
            along = [(gate_mid.at[slot, line(k)], gate_second.at[slot, k - 1]) for k in range(1, col_lines)]
        elif stage == 2:
            pair = (left.at[slot, 0, 0], left.at[slot, 0, 1])
            along = [(right.at[slot, 0, 0], right.at[slot, 0, k]) for k in range(1, col_lines)]
        else:
            pair = (right.at[slot, 0], right.at[slot, 1])
            along = [(left.at[slot, 0], left.at[slot, k]) for k in range(1, col_lines)]
        copies = [
            remote(*pair, pair_send.at[stage, slot], pair_recv.at[stage, slot], "col", col_other)
        ]
        for k in range(1, col_lines):
            copies.append(
                remote(
                    *along[k - 1],
                    line_send.at[stage, slot, k - 1],
                    line_recv.at[stage, slot, k - 1],
                    "col",
                    line(k) * 2 + pair_me,
                )
            )
        return copies

    for p in range(spare):
        wo_copy(p).start()
    for j in range(steps):
        gate_copy(j).start()
        up_copy(j).start()
        if j < steps - spare:
            down_copy(j).start()
    barrier = pltpu.get_barrier_semaphore()
    for k in range(1, cols):
        pl.semaphore_signal(
            barrier, inc=1, device_id={"col": lax.rem(col + k, cols)}, device_id_type=MESH
        )
    pl.semaphore_signal(barrier, inc=1, device_id={"row": row_other}, device_id_type=MESH)
    for k in range(1, row_lines):
        pl.semaphore_signal(
            barrier, inc=1, device_id={"row": layer(k) * 2 + core}, device_id_type=MESH
        )
    pl.semaphore_wait(barrier, cols - 1 + row_lines)
    for q in range(NC):
        for k in range(1, cols):
            att_copy(q, k).start()
    total[...] = jnp.zeros_like(total)
    for p in range(spare):
        wo_copy(p).wait()

    for q in range(NC):
        att_buf[q, col] = att_ref[:, q * toks : (q + 1) * toks, :]
        for k in range(1, cols):
            att_copy(q, k).wait()
        inputs = att_buf[q].reshape(many, att_buf.shape[-1])
        for start in range(0, width, tile):
            product = jnp.zeros((many, tile), jnp.float32)
            for p in range(spare):
                product = product + jnp.dot(
                    inputs[:, p * wide : (p + 1) * wide],
                    down_buf[steps - spare + p, :, start : start + tile],
                    preferred_element_type=jnp.float32,
                )
            part[0, q, :, :, :, start : start + tile] = product.astype(jnp.bfloat16).reshape(
                row_lines, 2, toks, tile
            )
        rs_pair(0, q).start()
        rs_middle(0, q)
        if q == 0:
            rs_lines_start(0, 0)
    for j in range(steps - spare, steps):
        down_copy(j).start()
    stream_step(0)
    norm_step(0)
    if NC > 1:
        rs_lines_start(0, 1)
    ag_forward(0)

    chunks = NC * steps

    def stage_when(i, stage):
        return pl.when((i >= stage) & (i < chunks + stage))

    def iteration(i, carry):
        q_now = i // steps
        j_now = lax.rem(i, steps)

        @pl.when((j_now == 0) & (q_now < NC))
        def _():
            ag_done(q_now)

        @stage_when(i, 0)
        def _():
            @pl.when(i < steps)
            def _():
                gate_copy(i).wait()
                up_copy(i).wait()

            slot = lax.rem(i, SLOTS)
            inputs = pieces[q_now].reshape(many, pieces.shape[-1])
            product = jnp.dot(inputs, gate_buf[j_now], preferred_element_type=jnp.float32).astype(jnp.bfloat16)
            for b in range(cols):
                gate_part[slot, b % 2, b // 2] = product[b * share : (b + 1) * share]
            product = jnp.dot(inputs, up_buf[j_now], preferred_element_type=jnp.float32).astype(jnp.bfloat16)
            for b in range(cols):
                up_part[slot, b // 2, b % 2] = product[b * share : (b + 1) * share]
            for copy in transfers(0, slot):
                copy.start()

        @stage_when(i, 1)
        def _():
            slot = lax.rem(i - 1, SLOTS)
            for copy in transfers(0, slot):
                copy.wait()
            gate_mid[slot] = (
                gate_part[slot, pair_me].astype(jnp.float32) + gate_first[slot].astype(jnp.float32)
            ).astype(jnp.bfloat16)
            up_sum = up_part[slot, line_me].astype(jnp.float32)
            for k in range(1, col_lines):
                up_sum = up_sum + up_first[slot, k - 1].astype(jnp.float32)
            up_mid[slot] = up_sum.astype(jnp.bfloat16)
            for copy in transfers(1, slot):
                copy.start()

        @stage_when(i, 2)
        def _():
            slot = lax.rem(i - 2, SLOTS)
            for copy in transfers(1, slot):
                copy.wait()
            gate = gate_mid[slot, line_me].astype(jnp.float32)
            for k in range(1, col_lines):
                gate = gate + gate_second[slot, k - 1].astype(jnp.float32)
            up = up_mid[slot, pair_me].astype(jnp.float32) + up_second[slot].astype(jnp.float32)
            hidden = (gate / (1.0 + jnp.exp(-gate)) * up).astype(jnp.bfloat16)
            left[slot, 0, 0] = hidden[:, :half]
            right[slot, 0, 0] = hidden[:, half:]
            for copy in transfers(2, slot):
                copy.start()

        @stage_when(i, 3)
        def _():
            slot = lax.rem(i - 3, SLOTS)
            for copy in transfers(2, slot):
                copy.wait()
            for copy in transfers(3, slot):
                copy.start()

        @stage_when(i, 4)
        def _():
            j = lax.rem(i - 4, steps)
            slot = lax.rem(i - 4, SLOTS)

            @pl.when(i - 4 < steps)
            def _():
                down_copy(i - 4).wait()

            for copy in transfers(3, slot):
                copy.wait()
            gathered = jnp.concatenate(
                [
                    jnp.concatenate([left[slot, k, p], right[slot, p, k]], axis=1)
                    for p in range(2)
                    for k in range(col_lines)
                ],
                axis=0,
            )
            for start in range(0, width, tile):
                total[:, start : start + tile] += jnp.dot(
                    gathered,
                    down_buf[j, :, start : start + tile],
                    preferred_element_type=jnp.float32,
                )

        @pl.when((j_now == 1) & (q_now + 1 < NC))
        def _():
            stream_step(q_now + 1)

        @pl.when((j_now == 2) & (q_now + 1 < NC))
        def _():
            norm_step(q_now + 1)

        @pl.when((j_now == 2) & (q_now + 2 < NC))
        def _():
            rs_lines_start(0, q_now + 2)

        @pl.when((j_now == 5) & (q_now + 1 < NC))
        def _():
            ag_forward(q_now + 1)

        @pl.when((i >= steps + 3) & (lax.rem(i - 3, steps) == 0))
        def _():
            q = (i - 4) // steps
            for p in range(2):
                for k in range(col_lines):
                    owner = line(col_lines - k) * 2 + lax.rem(pair_me + p, 2)
                    begin = (p * col_lines + k) * share
                    part[1, q, owner] = (
                        total[begin : begin + share, :].astype(jnp.bfloat16).reshape(2, toks, width)
                    )
            rs_pair(1, q).start()
            total[...] = jnp.zeros_like(total)

        @pl.when((i >= steps + 4) & (lax.rem(i - 4, steps) == 0))
        def _():
            q = (i - 5) // steps
            rs_middle(1, q)
            rs_lines_start(1, q)

        @pl.when((i >= steps + 8) & (lax.rem(i - 8, steps) == 0))
        def _():
            q = (i - 9) // steps
            out_ref[q] = stream[q] + rs_finish(1, q)

        return carry

    lax.fori_loop(0, chunks + 4, iteration, 0)
    rs_middle(1, NC - 1)
    rs_lines_start(1, NC - 1)
    out_ref[NC - 1] = stream[NC - 1] + rs_finish(1, NC - 1)


def tail(attended, out_weight, residual, norm_gain, gate_weight, up_weight, down_weight):
    cols = lax.axis_size("col")
    rows = lax.axis_size("row")
    depth, hidden_width = gate_weight.shape
    tokens, width = residual.shape
    inner = out_weight.shape[0]
    wide = hidden_width // STEPS
    toks = tokens // NC
    share = rows * toks // cols
    col_lines = cols // 2
    row_lines = rows // 2
    assert rows == 2 * cols and inner % wide == 0
    vmem = pl.BlockSpec(memory_space=pltpu.VMEM)
    hbm = pl.BlockSpec(memory_space=pl.ANY)
    dma = pltpu.SemaphoreType.DMA

    def held(*shape):
        return pltpu.VMEM(shape, jnp.bfloat16)

    out = pl.pallas_call(
        functools.partial(tail_kernel, cols, rows),
        out_shape=jax.ShapeDtypeStruct((NC, toks, width), jnp.float32),
        in_specs=[vmem, hbm, vmem, vmem, hbm, hbm, hbm],
        out_specs=vmem,
        scratch_shapes=[
            held(STEPS, depth, wide),
            held(STEPS, depth, wide),
            held(STEPS, wide, width),
            held(NC, cols, 2, toks, inner),
            held(2, NC, row_lines, 2, toks, width),
            held(2, NC, row_lines, toks, width),
            held(2, NC, row_lines, toks, width),
            held(2, NC, row_lines - 1, toks, width),
            pltpu.VMEM((NC, toks, width), jnp.float32),
            pltpu.VMEM((NC, toks, 128), jnp.float32),
            pltpu.VMEM((NC, cols - 1, toks, 128), jnp.float32),
            held(NC, row_lines, 2, toks, depth),
            held(SLOTS, 2, col_lines, share, wide),
            held(SLOTS, col_lines, 2, share, wide),
            held(SLOTS, col_lines, share, wide),
            held(SLOTS, col_lines - 1, 2, share, wide),
            held(SLOTS, col_lines, share, wide),
            held(SLOTS, 2, share, wide),
            held(SLOTS, col_lines - 1, share, wide),
            held(SLOTS, share, wide),
            held(SLOTS, col_lines, 2, share, wide // 2),
            held(SLOTS, 2, col_lines, share, wide // 2),
            pltpu.VMEM((cols * share, width), jnp.float32),
            dma((STEPS,)),
            dma((STEPS,)),
            dma((STEPS,)),
            dma((inner // wide,)),
            dma((NC, cols - 1)),
            dma((NC, cols - 1)),
            dma((2, NC)),
            dma((2, NC)),
            dma((2, NC, row_lines - 1)),
            dma((2, NC, row_lines - 1)),
            dma((NC, cols - 1)),
            dma((NC, cols - 1)),
            dma((NC, row_lines - 1)),
            dma((NC, row_lines - 1)),
            dma((NC, row_lines)),
            dma((NC, row_lines)),
            dma((4, SLOTS)),
            dma((4, SLOTS)),
            dma((4, SLOTS, col_lines - 1)),
            dma((4, SLOTS, col_lines - 1)),
        ],
        compiler_params=pltpu.CompilerParams(
            collective_id=0, has_side_effects=True, vmem_limit_bytes=66 * 1000 * 1000
        ),
    )(
        attended,
        out_weight,
        residual.reshape(NC, toks, width),
        norm_gain.reshape(1, width),
        gate_weight,
        up_weight,
        down_weight,
    )
    return out.reshape(tokens, width).astype(jnp.bfloat16)


def local(
    queries,
    cache_keys,
    cache_values,
    stretch_keys,
    stretch_values,
    block_lists,
    out_weight,
    residual,
    norm_gain,
    gate_weight,
    up_weight,
    down_weight,
):
    row_count = lax.axis_size("row")
    col_count = lax.axis_size("col")
    row_index = lax.axis_index("row")
    col_index = lax.axis_index("col")
    device_count = row_count * col_count
    my_index = row_index * col_count + col_index
    local_blocks = cache_keys.shape[1] // BLK
    heads_here = queries.shape[1] // HEAD_DIM
    lists = jnp.swapaxes(block_lists, 0, 1)
    lists = jnp.repeat(lists, row_count // KV_HEADS, axis=0).reshape(device_count, -1)
    matched = lists // local_blocks == my_index
    block_rows = jnp.sum(jnp.where(matched, lists % local_blocks, 0), axis=1)
    blocks = gather_blocks(block_rows, cache_keys, cache_values)
    my_list = block_lists[col_index, row_index * heads_here // GROUP]
    sources = jnp.arange(device_count, dtype=jnp.int32)
    wanted = jnp.any(my_list[None, :] // local_blocks == sources[:, None], axis=1)
    bias = jnp.broadcast_to(jnp.where(wanted, 0.0, -1e30)[:, None, None], (device_count, 1, BLK))
    attended = attend(queries, blocks, bias, stretch_keys, stretch_values, residual.shape[0])
    return tail(attended, out_weight, residual, norm_gain, gate_weight, up_weight, down_weight)


def solution(mesh):
    in_specs = (
        P("col", "row"),
        P(None, ("row", "col"), None),
        P(None, ("row", "col"), None),
        P(None, "col", None),
        P(None, "col", None),
        P(),
        P("row", "col"),
        P("row", "col"),
        P("col"),
        P("col", "row"),
        P("col", "row"),
        P("row", "col"),
    )
    out_specs = P("row", "col")
    return jax.shard_map(local, mesh=mesh, in_specs=in_specs, out_specs=out_specs, check_vma=False)
```

```python
import functools
import math

import jax
import jax.numpy as jnp
from jax import lax
from jax.experimental import pallas as pl
from jax.experimental.pallas import tpu as pltpu
from jax.sharding import PartitionSpec as P

KV_HEADS = 8
HEAD_DIM = 128
BLK = 128
GROUP = 8
SLOTS = 8
HOLD = 4
LAGS = (0, 2, 4, 6, 8)
MESH = pl.DeviceIdType.MESH
NC = 4
STEPS = 7


def gather_kernel(rows_ref, keys_ref, values_ref, out_ref, key_sem, value_sem):
    groups = keys_ref.shape[0]
    cols = rows_ref.shape[0]
    devices = out_ref.shape[0]

    def copies(d):
        group = d * groups // devices
        positions = pl.ds(pl.multiple_of(rows_ref[d % cols, group] * BLK, BLK), BLK)
        return (
            pltpu.make_async_copy(keys_ref.at[group, positions], out_ref.at[d, 0], key_sem.at[d]),
            pltpu.make_async_copy(values_ref.at[group, positions], out_ref.at[d, 1], value_sem.at[d]),
        )

    for d in range(devices):
        for copy in copies(d):
            copy.start()
    for d in range(devices):
        for copy in copies(d):
            copy.wait()


def gather_blocks(block_rows, cache_keys, cache_values, devices):
    dma = pltpu.SemaphoreType.DMA
    return pl.pallas_call(
        gather_kernel,
        out_shape=jax.ShapeDtypeStruct((devices, 2, BLK, HEAD_DIM), cache_keys.dtype),
        in_specs=[
            pl.BlockSpec(memory_space=pltpu.SMEM),
            pl.BlockSpec(memory_space=pl.ANY),
            pl.BlockSpec(memory_space=pl.ANY),
        ],
        out_specs=pl.BlockSpec(memory_space=pltpu.VMEM),
        scratch_shapes=[dma((devices,)), dma((devices,))],
        compiler_params=pltpu.CompilerParams(vmem_limit_bytes=63 * 1024 * 1024),
    )(block_rows, cache_keys, cache_values)


def flipped(index, bits):
    result = index
    place = 1
    while place <= bits:
        if bits // place % 2:
            result = result + place * (1 - 2 * lax.rem(index // place, 2))
        place *= 2
    return result


def attention(
    rows,
    cols,
    local_blocks,
    begin,
    query_ref,
    block_ref,
    lists_ref,
    near_key_ref,
    near_value_ref,
    out_ref,
    held,
    near,
    heads_first,
    top,
    norm,
    acc,
    near_sem,
    near_send,
    near_recv,
    block_send,
    block_recv,
):
    row = lax.axis_index("row")
    col = lax.axis_index("col")
    devices = rows * cols
    heads = query_ref.shape[1] // HEAD_DIM
    group = row * heads // GROUP
    scaling = 1.0 / math.sqrt(HEAD_DIM)
    pairs = heads // 2
    order = sorted(range(devices), key=lambda k: (k // cols // 2, k))
    slot_of = {k: s for s, k in enumerate(order)}

    def peer(k):
        return flipped(row, k // cols), flipped(col, k % cols)

    def block_copy(k):
        peer_row, peer_col = peer(k)
        slot = slot_of[k]
        return pltpu.make_async_remote_copy(
            src_ref=block_ref.at[peer_row * cols + peer_col],
            dst_ref=held.at[slot],
            send_sem=block_send.at[slot],
            recv_sem=block_recv.at[slot],
            device_id={"row": peer_row, "col": peer_col},
            device_id_type=MESH,
        )

    def near_copy(k):
        return pltpu.make_async_remote_copy(
            src_ref=near.at[col],
            dst_ref=near.at[col],
            send_sem=near_send.at[k - 1],
            recv_sem=near_recv.at[k - 1],
            device_id={"col": flipped(col, k)},
            device_id_type=MESH,
        )

    own = (
        pltpu.make_async_copy(near_key_ref.at[group], near.at[col, 0], near_sem.at[0]),
        pltpu.make_async_copy(near_value_ref.at[group], near.at[col, 1], near_sem.at[1]),
    )
    own_block = pltpu.make_async_copy(block_ref.at[row * cols + col], held.at[0], near_sem.at[2])
    for copy in own:
        copy.start()
    own_block.start()
    barrier = pltpu.get_barrier_semaphore()
    for k in range(1, devices):
        peer_row, peer_col = peer(k)
        pl.semaphore_signal(
            barrier, inc=1, device_id={"row": peer_row, "col": peer_col}, device_id_type=MESH
        )
    pl.semaphore_wait(barrier, devices - 1)
    for copy in own:
        copy.wait()
    for k in range(1, cols):
        near_copy(k).start()
    for k in order[1:]:
        block_copy(k).start()
    begin()
    for h in range(heads):
        heads_first[h * BLK : (h + 1) * BLK, :] = query_ref[:, h * HEAD_DIM : (h + 1) * HEAD_DIM]
    for k in range(1, cols):
        near_copy(k).wait()

    def near_pass(p, carry):
        lines = pl.ds(pl.multiple_of(p * 2 * BLK, 2 * BLK), 2 * BLK)
        keys = near[:, 0].reshape(cols * BLK, HEAD_DIM)
        scores = lax.dot_general(
            heads_first[lines, :], keys, (((1,), (1,)), ((), ())), preferred_element_type=jnp.float32
        ) * scaling
        position = lax.broadcasted_iota(jnp.int32, scores.shape, 1)
        token = col * BLK + lax.rem(lax.broadcasted_iota(jnp.int32, scores.shape, 0), BLK)
        allowed = position <= token
        scores = jnp.where(allowed, scores, -1e30)
        new_top = jnp.max(scores, axis=1, keepdims=True)
        weights = jnp.where(allowed, jnp.exp(scores - new_top), 0.0)
        top[lines, :] = jnp.broadcast_to(new_top, (2 * BLK, HEAD_DIM))
        norm[lines, :] = jnp.broadcast_to(jnp.sum(weights, axis=1, keepdims=True), (2 * BLK, HEAD_DIM))
        acc[lines, :] = jnp.dot(
            weights.astype(jnp.bfloat16),
            near[:, 1].reshape(cols * BLK, HEAD_DIM),
            preferred_element_type=jnp.float32,
        )
        return carry

    lax.fori_loop(0, pairs, near_pass, 0)

    listed = lists_ref[col, pl.ds(group, 1), :]

    def bias_of(source):
        inside = (listed >= source * local_blocks) & (listed < (source + 1) * local_blocks)
        found = jnp.max(jnp.where(inside, 1.0, 0.0), axis=1, keepdims=True)
        return jnp.broadcast_to(jnp.where(found > 0.5, 0.0, -1e30), (1, BLK))

    batch = 4
    for first in range(0, devices, batch):
        bias = []
        for slot in range(first, first + batch):
            k = order[slot]
            if k:
                block_copy(k).wait()
            else:
                own_block.wait()
            peer_row, peer_col = peer(k)
            bias.append(bias_of(peer_row * cols + peer_col))
        bias = jnp.concatenate(bias, axis=1)

        def far_pass(p, carry):
            lines = pl.ds(pl.multiple_of(p * 2 * BLK, 2 * BLK), 2 * BLK)
            keys = held[first : first + batch, 0].reshape(batch * BLK, HEAD_DIM)
            scores = (
                lax.dot_general(
                    heads_first[lines, :], keys, (((1,), (1,)), ((), ())), preferred_element_type=jnp.float32
                )
                * scaling
                + bias
            )
            old_top = top[lines, :]
            new_top = jnp.maximum(old_top, jnp.max(scores, axis=1, keepdims=True))
            decay = jnp.exp(old_top - new_top)
            weights = jnp.exp(scores - new_top[:, :1])
            top[lines, :] = new_top
            norm[lines, :] = norm[lines, :] * decay + jnp.sum(weights, axis=1, keepdims=True)
            acc[lines, :] = acc[lines, :] * decay + jnp.dot(
                weights.astype(jnp.bfloat16),
                held[first : first + batch, 1].reshape(batch * BLK, HEAD_DIM),
                preferred_element_type=jnp.float32,
            )
            return carry

        lax.fori_loop(0, pairs, far_pass, 0)
    halves = out_ref.shape[1]
    for h in range(heads):
        lines = slice(h * BLK, (h + 1) * BLK)
        result = (acc[lines, :] / norm[lines, :]).astype(jnp.bfloat16)
        for p in range(BLK // halves):
            out_ref[p, :, h * HEAD_DIM : (h + 1) * HEAD_DIM] = result[p * halves : (p + 1) * halves]


def layer_kernel(
    cols,
    rows,
    local_blocks,
    query_ref,
    block_ref,
    lists_ref,
    near_key_ref,
    near_value_ref,
    wo_ref,
    res_ref,
    gain_ref,
    gate_ref,
    up_ref,
    down_ref,
    out_ref,
    gate_buf,
    up_buf,
    down_buf,
    held,
    near,
    heads_first,
    top,
    norm,
    acc,
    att_ref,
    att_buf,
    part,
    first,
    mid,
    second,
    stream,
    square_own,
    square_buf,
    pieces,
    gate_part,
    up_part,
    gate_first,
    up_first,
    gate_mid,
    up_mid,
    gate_second,
    up_second,
    left,
    right,
    total,
    gate_sem,
    up_sem,
    down_sem,
    wo_sem,
    near_sem,
    near_send,
    near_recv,
    block_send,
    block_recv,
    att_send,
    att_recv,
    rs_pair_send,
    rs_pair_recv,
    rs_line_send,
    rs_line_recv,
    square_send,
    square_recv,
    ag_line_send,
    ag_line_recv,
    ag_pair_send,
    ag_pair_recv,
    pair_send,
    pair_recv,
    line_send,
    line_recv,
):
    col = lax.axis_index("col")
    row = lax.axis_index("row")
    steps = gate_buf.shape[0]
    wide = gate_buf.shape[2]
    half = wide // 2
    share = gate_part.shape[3]
    _, toks, width = out_ref.shape
    many = cols * share
    spare = wo_ref.shape[0] // wide
    tile = min(512, width)
    col_lines = cols // 2
    pair_me = lax.rem(col, 2)
    line_me = col // 2
    col_other = line_me * 2 + (1 - pair_me)
    row_lines = rows // 2
    core = lax.rem(row, 2)
    depth_me = row // 2
    row_other = depth_me * 2 + (1 - core)

    def line(k):
        return lax.rem(line_me + k, col_lines)

    def layer(k):
        return lax.rem(depth_me + k, row_lines)

    def remote(src, dst, send, recv, axis, device):
        return pltpu.make_async_remote_copy(
            src_ref=src,
            dst_ref=dst,
            send_sem=send,
            recv_sem=recv,
            device_id={axis: device},
            device_id_type=MESH,
        )

    def gate_copy(j):
        return pltpu.make_async_copy(
            gate_ref.at[:, pl.ds(pl.multiple_of(j * wide, wide), wide)], gate_buf.at[j], gate_sem.at[j]
        )

    def up_copy(j):
        return pltpu.make_async_copy(
            up_ref.at[:, pl.ds(pl.multiple_of(j * wide, wide), wide)], up_buf.at[j], up_sem.at[j]
        )

    def down_copy(j):
        return pltpu.make_async_copy(
            down_ref.at[pl.ds(pl.multiple_of(j * wide, wide), wide), :], down_buf.at[j], down_sem.at[j]
        )

    def wo_copy(p):
        return pltpu.make_async_copy(
            wo_ref.at[p * wide : (p + 1) * wide, :], down_buf.at[steps - spare + p], wo_sem.at[p]
        )

    def att_copy(q, k):
        return remote(
            att_ref.at[:, q * toks : (q + 1) * toks, :],
            att_buf.at[q, col],
            att_send.at[q, k - 1],
            att_recv.at[q, k - 1],
            "col",
            lax.rem(col + k, cols),
        )

    def rs_pair(w, q):
        return remote(
            part.at[q, :, 1 - core],
            first.at[q],
            rs_pair_send.at[w, q],
            rs_pair_recv.at[w, q],
            "row",
            row_other,
        )

    def rs_line(w, q, k):
        return remote(
            mid.at[q, layer(k)],
            second.at[q, k - 1],
            rs_line_send.at[w, q, k - 1],
            rs_line_recv.at[w, q, k - 1],
            "row",
            layer(k) * 2 + core,
        )

    def rs_middle(w, q):
        rs_pair(w, q).wait()
        for d in range(row_lines):
            mid[q, d] = (
                part[q, d, core].astype(jnp.float32) + first[q, d].astype(jnp.float32)
            ).astype(jnp.bfloat16)

    def rs_lines_start(w, q):
        for k in range(1, row_lines):
            rs_line(w, q, k).start()

    def rs_finish(w, q):
        result = mid[q, depth_me].astype(jnp.float32)
        for k in range(1, row_lines):
            rs_line(w, q, k).wait()
            result = result + second[q, k - 1].astype(jnp.float32)
        return result

    def square_copy(q, k):
        return remote(
            square_own.at[q],
            square_buf.at[q, k - 1],
            square_send.at[q, k - 1],
            square_recv.at[q, k - 1],
            "col",
            lax.rem(col + k, cols),
        )

    def stream_step(q):
        value = rs_finish(0, q) + res_ref[q].astype(jnp.float32)
        stream[q] = value
        squares = jnp.sum(value * value, axis=1, keepdims=True)
        square_own[q] = jnp.broadcast_to(squares, (toks, 128))
        for k in range(1, cols):
            square_copy(q, k).start()

    def ag_line(q, k):
        return remote(
            pieces.at[q, depth_me, core],
            pieces.at[q, depth_me, core],
            ag_line_send.at[q, k - 1],
            ag_line_recv.at[q, k - 1],
            "row",
            layer(k) * 2 + core,
        )

    def ag_pair(q, k):
        owner = layer(row_lines - k)
        return remote(
            pieces.at[q, owner, core],
            pieces.at[q, owner, core],
            ag_pair_send.at[q, k],
            ag_pair_recv.at[q, k],
            "row",
            row_other,
        )

    def norm_step(q):
        squares = square_own[q]
        for k in range(1, cols):
            square_copy(q, k).wait()
            squares = squares + square_buf[q, k - 1]
        factor = lax.rsqrt(squares / (width * cols) + 1e-05)[:, :1]
        pieces[q, depth_me, core] = (stream[q] * factor * gain_ref[...].astype(jnp.float32)[None, :]).astype(
            jnp.bfloat16
        )
        for k in range(1, row_lines):
            ag_line(q, k).start()
        ag_pair(q, 0).start()

    def ag_forward(q):
        for k in range(1, row_lines):
            ag_line(q, k).wait()
            ag_pair(q, k).start()

    def ag_done(q):
        for k in range(row_lines):
            ag_pair(q, k).wait()

    def transfers(stage, step):
        slot = lax.rem(step, SLOTS)
        hold = lax.rem(step, HOLD)
        if stage == 0:
            pair = (gate_part.at[hold, 1 - pair_me], gate_first.at[slot])
            along = [(up_part.at[hold, line(k)], up_first.at[slot, k - 1]) for k in range(1, col_lines)]
        elif stage == 1:
            pair = (up_mid.at[hold, 1 - pair_me], up_second.at[slot])
            along = [(gate_mid.at[hold, line(k)], gate_second.at[slot, k - 1]) for k in range(1, col_lines)]
        elif stage == 2:
            pair = (left.at[slot, 0, 0], left.at[slot, 0, 1])
            along = [(right.at[slot, 0, 0], right.at[slot, 0, k]) for k in range(1, col_lines)]
        else:
            pair = (right.at[slot, 0], right.at[slot, 1])
            along = [(left.at[slot, 0], left.at[slot, k]) for k in range(1, col_lines)]
        copies = [
            remote(*pair, pair_send.at[stage, slot], pair_recv.at[stage, slot], "col", col_other)
        ]
        for k in range(1, col_lines):
            copies.append(
                remote(
                    *along[k - 1],
                    line_send.at[stage, slot, k - 1],
                    line_recv.at[stage, slot, k - 1],
                    "col",
                    line(k) * 2 + pair_me,
                )
            )
        return copies

    for p in range(spare):
        wo_copy(p).start()

    def begin():
        for j in range(steps):
            gate_copy(j).start()
            up_copy(j).start()
        for j in range(steps - spare):
            down_copy(j).start()

    attention(
        rows,
        cols,
        local_blocks,
        begin,
        query_ref,
        block_ref,
        lists_ref,
        near_key_ref,
        near_value_ref,
        att_ref,
        held,
        near,
        heads_first,
        top,
        norm,
        acc,
        near_sem,
        near_send,
        near_recv,
        block_send,
        block_recv,
    )
    for q in range(NC):
        for k in range(1, cols):
            att_copy(q, k).start()
    total[...] = jnp.zeros_like(total)
    for p in range(spare):
        wo_copy(p).wait()

    def project(q):
        att_buf[q, col] = att_ref[:, q * toks : (q + 1) * toks, :]
        for k in range(1, cols):
            att_copy(q, k).wait()
        inputs = att_buf[q].reshape(many, att_buf.shape[-1])
        for start in range(0, width, tile):
            product = jnp.zeros((many, tile), jnp.float32)
            for p in range(spare):
                product = product + jnp.dot(
                    inputs[:, p * wide : (p + 1) * wide],
                    down_buf[steps - spare + p, :, start : start + tile],
                    preferred_element_type=jnp.float32,
                )
            part[q, :, :, :, start : start + tile] = product.astype(jnp.bfloat16).reshape(
                row_lines, 2, toks, tile
            )
        rs_pair(0, q).start()

    project(0)
    rs_middle(0, 0)
    rs_lines_start(0, 0)
    project(1)
    rs_middle(0, 1)
    rs_lines_start(0, 1)
    stream_step(0)
    norm_step(0)
    stream_step(1)
    norm_step(1)
    for q in range(2, NC):
        project(q)
    for j in range(steps - spare, steps):
        down_copy(j).start()
    for q in range(2, NC):
        rs_middle(0, q)
    ag_forward(0)
    rs_lines_start(0, 2)

    chunks = NC * steps

    def stage_when(i, stage):
        return pl.when((i >= LAGS[stage]) & (i < chunks + LAGS[stage]))

    def iteration(i, carry):
        q_now = i // steps
        j_now = lax.rem(i, steps)

        @pl.when((j_now == 0) & (q_now < NC))
        def _():
            ag_done(q_now)

        @stage_when(i, 0)
        def _():
            @pl.when(i < steps)
            def _():
                gate_copy(i).wait()
                up_copy(i).wait()

            hold = lax.rem(i, HOLD)
            inputs = pieces[q_now].reshape(many, pieces.shape[-1])
            product = jnp.dot(inputs, gate_buf[j_now], preferred_element_type=jnp.float32).astype(jnp.bfloat16)
            for b in range(cols):
                gate_part[hold, b % 2, b // 2] = product[b * share : (b + 1) * share]
            product = jnp.dot(inputs, up_buf[j_now], preferred_element_type=jnp.float32).astype(jnp.bfloat16)
            for b in range(cols):
                up_part[hold, b // 2, b % 2] = product[b * share : (b + 1) * share]
            for copy in transfers(0, i):
                copy.start()

        @stage_when(i, 1)
        def _():
            step = i - LAGS[1]
            slot = lax.rem(step, SLOTS)
            hold = lax.rem(step, HOLD)
            for copy in transfers(0, step):
                copy.wait()
            gate_mid[hold] = (
                gate_part[hold, pair_me].astype(jnp.float32) + gate_first[slot].astype(jnp.float32)
            ).astype(jnp.bfloat16)
            up_sum = up_part[hold, line_me].astype(jnp.float32)
            for k in range(1, col_lines):
                up_sum = up_sum + up_first[slot, k - 1].astype(jnp.float32)
            up_mid[hold] = up_sum.astype(jnp.bfloat16)
            for copy in transfers(1, step):
                copy.start()

        @stage_when(i, 2)
        def _():
            step = i - LAGS[2]
            slot = lax.rem(step, SLOTS)
            hold = lax.rem(step, HOLD)
            for copy in transfers(1, step):
                copy.wait()
            gate = gate_mid[hold, line_me].astype(jnp.float32)
            for k in range(1, col_lines):
                gate = gate + gate_second[slot, k - 1].astype(jnp.float32)
            up = up_mid[hold, pair_me].astype(jnp.float32) + up_second[slot].astype(jnp.float32)
            hidden = (gate / (1.0 + jnp.exp(-gate)) * up).astype(jnp.bfloat16)
            left[slot, 0, 0] = hidden[:, :half]
            right[slot, 0, 0] = hidden[:, half:]
            for copy in transfers(2, step):
                copy.start()

        @stage_when(i, 3)
        def _():
            for copy in transfers(2, i - LAGS[3]):
                copy.wait()
            for copy in transfers(3, i - LAGS[3]):
                copy.start()

        @stage_when(i, 4)
        def _():
            step = i - LAGS[4]
            j = lax.rem(step, steps)
            slot = lax.rem(step, SLOTS)

            @pl.when(step < steps)
            def _():
                down_copy(step).wait()

            for copy in transfers(3, step):
                copy.wait()
            gathered = jnp.concatenate(
                [
                    jnp.concatenate([left[slot, k, p], right[slot, p, k]], axis=1)
                    for p in range(2)
                    for k in range(col_lines)
                ],
                axis=0,
            )
            for start in range(0, width, tile):
                total[:, start : start + tile] += jnp.dot(
                    gathered,
                    down_buf[j, :, start : start + tile],
                    preferred_element_type=jnp.float32,
                )

        @pl.when((j_now == 1) & (q_now + 2 < NC))
        def _():
            stream_step(q_now + 2)

        @pl.when((j_now == 2) & (q_now + 2 < NC))
        def _():
            norm_step(q_now + 2)

        @pl.when((j_now == 2) & (q_now + 3 < NC))
        def _():
            rs_lines_start(0, q_now + 3)

        @pl.when((j_now == 4) & (q_now + 1 < NC))
        def _():
            ag_forward(q_now + 1)

        done = i - LAGS[4] + 1
        q_done = done // steps - 1

        @pl.when((done > 0) & (lax.rem(done, steps) == 0))
        def _():
            for p in range(2):
                for k in range(col_lines):
                    owner = line(col_lines - k) * 2 + lax.rem(pair_me + p, 2)
                    begin = (p * col_lines + k) * share
                    part[q_done, owner] = (
                        total[begin : begin + share, :].astype(jnp.bfloat16).reshape(2, toks, width)
                    )
            rs_pair(1, q_done).start()
            total[...] = jnp.zeros_like(total)

        @pl.when((done > steps) & (lax.rem(done, steps) == 1))
        def _():
            rs_middle(1, q_done)
            rs_lines_start(1, q_done)

        @pl.when((done > steps) & (lax.rem(done, steps) == 5))
        def _():
            out_ref[q_done] = stream[q_done] + rs_finish(1, q_done)

        return carry

    lax.fori_loop(0, chunks + LAGS[4], iteration, 0)
    rs_middle(1, NC - 1)
    rs_lines_start(1, NC - 1)
    out_ref[NC - 1] = stream[NC - 1] + rs_finish(1, NC - 1)


def layer_call(
    queries,
    blocks,
    block_lists,
    local_blocks,
    stretch_keys,
    stretch_values,
    out_weight,
    residual,
    norm_gain,
    gate_weight,
    up_weight,
    down_weight,
):
    cols = lax.axis_size("col")
    rows = lax.axis_size("row")
    depth, hidden_width = gate_weight.shape
    tokens, width = residual.shape
    inner = out_weight.shape[0]
    wide = hidden_width // STEPS
    toks = tokens // NC
    share = rows * toks // cols
    col_lines = cols // 2
    row_lines = rows // 2
    devices = rows * cols
    lines = BLK * inner // HEAD_DIM
    assert rows == 2 * cols and inner % wide == 0
    vmem = pl.BlockSpec(memory_space=pltpu.VMEM)
    hbm = pl.BlockSpec(memory_space=pl.ANY)
    dma = pltpu.SemaphoreType.DMA

    def held(*shape):
        return pltpu.VMEM(shape, jnp.bfloat16)

    out = pl.pallas_call(
        functools.partial(layer_kernel, cols, rows, local_blocks),
        out_shape=jax.ShapeDtypeStruct((NC, toks, width), jnp.float32),
        in_specs=[vmem, hbm, vmem, hbm, hbm, hbm, vmem, vmem, hbm, hbm, hbm],
        out_specs=vmem,
        scratch_shapes=[
            held(STEPS, depth, wide),
            held(STEPS, depth, wide),
            held(STEPS, wide, width),
            held(devices, 2, BLK, HEAD_DIM),
            held(cols, 2, BLK, HEAD_DIM),
            held(lines, HEAD_DIM),
            pltpu.VMEM((lines, HEAD_DIM), jnp.float32),
            pltpu.VMEM((lines, HEAD_DIM), jnp.float32),
            pltpu.VMEM((lines, HEAD_DIM), jnp.float32),
            held(BLK // tokens, tokens, inner),
            held(NC, cols, 2, toks, inner),
            held(NC, row_lines, 2, toks, width),
            held(NC, row_lines, toks, width),
            held(NC, row_lines, toks, width),
            held(NC, row_lines - 1, toks, width),
            pltpu.VMEM((NC, toks, width), jnp.float32),
            pltpu.VMEM((NC, toks, 128), jnp.float32),
            pltpu.VMEM((NC, cols - 1, toks, 128), jnp.float32),
            held(NC, row_lines, 2, toks, depth),
            held(HOLD, 2, col_lines, share, wide),
            held(HOLD, col_lines, 2, share, wide),
            held(SLOTS, col_lines, share, wide),
            held(SLOTS, col_lines - 1, 2, share, wide),
            held(HOLD, col_lines, share, wide),
            held(HOLD, 2, share, wide),
            held(SLOTS, col_lines - 1, share, wide),
            held(SLOTS, share, wide),
            held(SLOTS, col_lines, 2, share, wide // 2),
            held(SLOTS, 2, col_lines, share, wide // 2),
            pltpu.VMEM((cols * share, width), jnp.float32),
            dma((STEPS,)),
            dma((STEPS,)),
            dma((STEPS,)),
            dma((inner // wide,)),
            dma((3,)),
            dma((cols - 1,)),
            dma((cols - 1,)),
            dma((devices,)),
            dma((devices,)),
            dma((NC, cols - 1)),
            dma((NC, cols - 1)),
            dma((2, NC)),
            dma((2, NC)),
            dma((2, NC, row_lines - 1)),
            dma((2, NC, row_lines - 1)),
            dma((NC, cols - 1)),
            dma((NC, cols - 1)),
            dma((NC, row_lines - 1)),
            dma((NC, row_lines - 1)),
            dma((NC, row_lines)),
            dma((NC, row_lines)),
            dma((4, SLOTS)),
            dma((4, SLOTS)),
            dma((4, SLOTS, col_lines - 1)),
            dma((4, SLOTS, col_lines - 1)),
        ],
        compiler_params=pltpu.CompilerParams(
            collective_id=0, has_side_effects=True, vmem_limit_bytes=66 * 1000 * 1000
        ),
    )(
        queries,
        blocks,
        block_lists,
        stretch_keys,
        stretch_values,
        out_weight,
        residual.reshape(NC, toks, width),
        norm_gain,
        gate_weight,
        up_weight,
        down_weight,
    )
    return out.reshape(tokens, width).astype(jnp.bfloat16)


def local(
    queries,
    cache_keys,
    cache_values,
    stretch_keys,
    stretch_values,
    block_lists,
    out_weight,
    residual,
    norm_gain,
    gate_weight,
    up_weight,
    down_weight,
):
    row_count = lax.axis_size("row")
    col_count = lax.axis_size("col")
    row_index = lax.axis_index("row")
    col_index = lax.axis_index("col")
    device_count = row_count * col_count
    my_index = row_index * col_count + col_index
    local_blocks = cache_keys.shape[1] // BLK
    matched = block_lists // local_blocks == my_index
    block_rows = jnp.sum(jnp.where(matched, block_lists % local_blocks, 0), axis=2)
    blocks = gather_blocks(block_rows, cache_keys, cache_values, device_count)
    return layer_call(
        queries,
        blocks,
        block_lists,
        local_blocks,
        stretch_keys,
        stretch_values,
        out_weight,
        residual,
        norm_gain,
        gate_weight,
        up_weight,
        down_weight,
    )


def solution(mesh):
    in_specs = (
        P("col", "row"),
        P(None, ("row", "col"), None),
        P(None, ("row", "col"), None),
        P(None, "col", None),
        P(None, "col", None),
        P(),
        P("row", "col"),
        P("row", "col"),
        P("col"),
        P("col", "row"),
        P("col", "row"),
        P("row", "col"),
    )
    out_specs = P("row", "col")
    return jax.shard_map(local, mesh=mesh, in_specs=in_specs, out_specs=out_specs, check_vma=False)
```

```python
import functools
import math

import jax
import jax.numpy as jnp
from jax import lax
from jax.experimental import pallas as pl
from jax.experimental.pallas import tpu as pltpu
from jax.sharding import PartitionSpec as P

KV_HEADS = 8
HEAD_DIM = 128
BLK = 128
GROUP = 8
SLOTS = 8
HOLD = 4
LAGS = (0, 2, 4, 6, 8)
MESH = pl.DeviceIdType.MESH
NC = 4
STEPS = 7


def gather_kernel(rows_ref, keys_ref, values_ref, out_ref, key_sem, value_sem):
    groups = keys_ref.shape[0]
    cols = rows_ref.shape[0]
    devices = out_ref.shape[0]

    def copies(d):
        group = d * groups // devices
        positions = pl.ds(pl.multiple_of(rows_ref[d % cols, group] * BLK, BLK), BLK)
        return (
            pltpu.make_async_copy(keys_ref.at[group, positions], out_ref.at[d, 0], key_sem.at[d]),
            pltpu.make_async_copy(values_ref.at[group, positions], out_ref.at[d, 1], value_sem.at[d]),
        )

    for d in range(devices):
        for copy in copies(d):
            copy.start()
    for d in range(devices):
        for copy in copies(d):
            copy.wait()


def gather_blocks(block_rows, cache_keys, cache_values, devices):
    dma = pltpu.SemaphoreType.DMA
    return pl.pallas_call(
        gather_kernel,
        out_shape=jax.ShapeDtypeStruct((devices, 2, BLK, HEAD_DIM), cache_keys.dtype),
        in_specs=[
            pl.BlockSpec(memory_space=pltpu.SMEM),
            pl.BlockSpec(memory_space=pl.ANY),
            pl.BlockSpec(memory_space=pl.ANY),
        ],
        out_specs=pl.BlockSpec(memory_space=pltpu.VMEM),
        scratch_shapes=[dma((devices,)), dma((devices,))],
        compiler_params=pltpu.CompilerParams(vmem_limit_bytes=63 * 1024 * 1024),
    )(block_rows, cache_keys, cache_values)


def flipped(index, bits):
    result = index
    place = 1
    while place <= bits:
        if bits // place % 2:
            result = result + place * (1 - 2 * lax.rem(index // place, 2))
        place *= 2
    return result


def attention(
    rows,
    cols,
    local_blocks,
    begin,
    query_ref,
    block_ref,
    lists_ref,
    near_key_ref,
    near_value_ref,
    out_ref,
    held,
    near,
    turned,
    top,
    norm,
    acc,
    stats,
    near_sem,
    near_send,
    near_recv,
    block_send,
    block_recv,
    swap_send,
    swap_recv,
):
    row = lax.axis_index("row")
    col = lax.axis_index("col")
    devices = rows * cols
    layers = rows // 2
    plane = 2 * cols
    depth = row // 2
    core = lax.rem(row, 2)
    low = layers // 2 - 1
    high = layers // 2
    heads = query_ref.shape[1] // HEAD_DIM
    scaling = 1.0 / math.sqrt(HEAD_DIM)
    lines = heads * BLK
    strip = min(256, lines)

    def is_middle(d):
        return jnp.where((d == low) | (d == high), 1, 0)

    paired = is_middle(depth)
    my_middle = low + depth // high
    mirror_row = (layers - 1 - depth) * 2 + core

    def differing(index, bits, size):
        result = 0
        place = 1
        while place < size:
            one = lax.rem(index // place, 2)
            two = lax.rem(bits // place, 2)
            result = result + place * (one + two - 2 * one * two)
            place *= 2
        return result

    def block_parts(kz, e):
        target_depth = flipped(depth, kz)
        target_core = flipped(core, e // cols)
        target_col = flipped(col, e % cols)
        host = target_depth + is_middle(target_depth) * (my_middle - target_depth)
        block = (target_depth * 2 + target_core) * cols + target_col
        return block, host * 2 + target_core, target_col, kz * plane + e

    def block_copy(kz, e):
        block, host_row, host_col, slot = block_parts(kz, e)
        return pltpu.make_async_remote_copy(
            src_ref=block_ref.at[block],
            dst_ref=held.at[slot],
            send_sem=block_send.at[slot],
            recv_sem=block_recv.at[slot],
            device_id={"row": host_row, "col": host_col},
            device_id_type=MESH,
        )

    def own_block(kz):
        block, _, _, slot = block_parts(kz, 0)
        return pltpu.make_async_copy(block_ref.at[block], held.at[slot], block_recv.at[slot])

    def arrived(slot):
        return pltpu.make_async_copy(block_ref.at[0], held.at[slot], block_recv.at[slot])

    def near_copy(k):
        return pltpu.make_async_remote_copy(
            src_ref=near.at[col],
            dst_ref=near.at[col],
            send_sem=near_send.at[k - 1],
            recv_sem=near_recv.at[k - 1],
            device_id={"col": flipped(col, k)},
            device_id_type=MESH,
        )

    def swap(src, dst, index):
        return pltpu.make_async_remote_copy(
            src_ref=src,
            dst_ref=dst,
            send_sem=swap_send.at[index],
            recv_sem=swap_recv.at[index],
            device_id={"row": mirror_row},
            device_id_type=MESH,
        )

    query_swap = swap(turned.at[0], turned.at[1], 0)
    result_swap = swap(turned.at[1], turned.at[2], 1)
    stats_swap = swap(stats.at[0], stats.at[1], 2)

    group = row * heads // GROUP
    own = (
        pltpu.make_async_copy(near_key_ref.at[group], near.at[col, 0], near_sem.at[0]),
        pltpu.make_async_copy(near_value_ref.at[group], near.at[col, 1], near_sem.at[1]),
    )
    for copy in own:
        copy.start()
    for h in range(heads):
        block = query_ref[:, h * HEAD_DIM : (h + 1) * HEAD_DIM].astype(jnp.float32)
        turned[0, :, h * BLK : (h + 1) * BLK] = jnp.transpose(block).astype(jnp.bfloat16)
    barrier = pltpu.get_barrier_semaphore()
    for k in range(1, devices):
        pl.semaphore_signal(
            barrier,
            inc=1,
            device_id={"row": flipped(row, k // cols), "col": flipped(col, k % cols)},
            device_id_type=MESH,
        )
    pl.semaphore_wait(barrier, devices - 1)

    @pl.when(paired == 1)
    def _():
        query_swap.start()

    for kz in list(range(high, layers)) + list(range(high)):
        for e in range(plane):
            if e:
                block_copy(kz, e).start()
            elif kz == 0:
                own_block(0).start()
            elif kz == layers - 1:

                @pl.when(paired == 1)
                def _():
                    own_block(layers - 1).start()

                @pl.when(paired == 0)
                def _():
                    block_copy(layers - 1, 0).start()
            else:
                block_copy(kz, e).start()
    for copy in own:
        copy.wait()
    for k in range(1, cols):
        near_copy(k).start()
    begin()
    top[1] = jnp.full(top.shape[1:], -1e30, jnp.float32)
    norm[1] = jnp.zeros(norm.shape[1:], jnp.float32)
    acc[1] = jnp.zeros(acc.shape[1:], jnp.float32)
    for k in range(1, cols):
        near_copy(k).wait()

    def weighted(values, weights):
        return lax.dot_general(
            values,
            weights.astype(jnp.bfloat16),
            (((0,), (0,)), ((), ())),
            preferred_element_type=jnp.float32,
        )

    near_keys = near[:, 0].reshape(cols * BLK, HEAD_DIM)
    near_values = near[:, 1].reshape(cols * BLK, HEAD_DIM)
    for begin_at in range(0, lines, strip):
        part = slice(begin_at, begin_at + strip)
        scores = jnp.dot(near_keys, turned[0, :, part], preferred_element_type=jnp.float32) * scaling
        position = lax.broadcasted_iota(jnp.int32, scores.shape, 0)
        token = col * BLK + lax.rem(lax.broadcasted_iota(jnp.int32, scores.shape, 1), BLK)
        allowed = position <= token
        scores = jnp.where(allowed, scores, -1e30)
        new_top = jnp.max(scores, axis=0, keepdims=True)
        weights = jnp.where(allowed, jnp.exp(scores - new_top), 0.0)
        top[0, :, part] = new_top
        norm[0, :, part] = jnp.sum(weights, axis=0, keepdims=True)
        acc[0, :, part] = weighted(near_values, weights)

    batch = 4
    turns = plane // batch

    @pl.when(paired == 1)
    def _():
        query_swap.wait()

    def far_batch(index, carry):
        turn = index // turns
        kz = lax.rem(turn + high, layers)
        first = kz * plane + lax.rem(index, turns) * batch
        shared = paired * (kz // high)
        problem_row = row + shared * (mirror_row - row)
        listed = lists_ref[col, pl.ds(problem_row * heads // GROUP, 1), :]
        source_depth = differing(depth, kz + shared * (layers - 1 - 2 * kz), layers)
        bias = []
        for j in range(batch):
            e = lax.rem(first + j, plane)
            source = (source_depth * 2 + differing(core, e // cols, 2)) * cols + differing(
                col, lax.rem(e, cols), cols
            )
            inside = (listed >= source * local_blocks) & (listed < (source + 1) * local_blocks)
            found = jnp.max(jnp.where(inside, 1.0, 0.0), axis=1, keepdims=True)
            bias.append(jnp.broadcast_to(jnp.where(found > 0.5, 0.0, -1e30), (BLK, strip)))
        bias = jnp.concatenate(bias, axis=0)
        for j in range(batch):
            arrived(first + j).wait()

        keys = held[pl.ds(first, batch), 0].reshape(batch * BLK, HEAD_DIM)
        values = held[pl.ds(first, batch), 1].reshape(batch * BLK, HEAD_DIM)
        parts = [slice(begin_at, begin_at + strip) for begin_at in range(0, lines, strip)]
        tops, norms, accs = [], [], []
        for part in parts:
            scores = jnp.dot(keys, turned[shared, :, part], preferred_element_type=jnp.float32) * scaling + bias
            old_top = top[shared, :, part]
            new_top = jnp.maximum(old_top, jnp.max(scores, axis=0, keepdims=True))
            decay = jnp.exp(old_top - new_top)
            weights = jnp.exp(scores - new_top)
            tops.append(new_top)
            norms.append(norm[shared, :, part] * decay + jnp.sum(weights, axis=0, keepdims=True))
            accs.append(acc[shared, :, part] * decay + weighted(values, weights))
        for n, part in enumerate(parts):
            top[shared, :, part] = tops[n]
            norm[shared, :, part] = norms[n]
            acc[shared, :, part] = accs[n]
        return carry

    lax.fori_loop(0, (layers - high) * turns, far_batch, 0)

    @pl.when(paired == 1)
    def _():
        turned[1] = (acc[1] / norm[1]).astype(jnp.bfloat16)
        stats[0, 0:1, :] = top[1]
        stats[0, 1:2, :] = norm[1]
        stats_swap.start()
        result_swap.start()

    lax.fori_loop((layers - high) * turns, layers * turns, far_batch, 0)

    @pl.when(paired == 1)
    def _():
        stats_swap.wait()
        result_swap.wait()
        other_top = stats[1, 0:1, :]
        own_top = top[0]
        both = jnp.maximum(own_top, other_top)
        own_part = jnp.exp(own_top - both)
        other_part = jnp.exp(other_top - both) * stats[1, 1:2, :]
        norm[0] = norm[0] * own_part + other_part
        acc[0] = acc[0] * own_part + turned[2].astype(jnp.float32) * other_part

    halves = out_ref.shape[1]
    for h in range(heads):
        part = slice(h * BLK, (h + 1) * BLK)
        result = jnp.transpose(acc[0, :, part] / norm[0, :, part]).astype(jnp.bfloat16)
        for p in range(BLK // halves):
            out_ref[p, :, h * HEAD_DIM : (h + 1) * HEAD_DIM] = result[p * halves : (p + 1) * halves]

    def finish():
        for kz in range(layers):
            for e in range(plane):
                if e or kz not in (0, layers - 1):
                    block_copy(kz, e).wait_send()

        @pl.when(paired == 0)
        def _():
            block_copy(layers - 1, 0).wait_send()

    return finish


def layer_kernel(
    cols,
    rows,
    local_blocks,
    query_ref,
    block_ref,
    lists_ref,
    near_key_ref,
    near_value_ref,
    wo_ref,
    res_ref,
    gain_ref,
    gate_ref,
    up_ref,
    down_ref,
    out_ref,
    gate_buf,
    up_buf,
    down_buf,
    held,
    near,
    turned,
    top,
    norm,
    acc,
    stats,
    att_ref,
    att_buf,
    part,
    first,
    mid,
    second,
    stream,
    square_own,
    square_buf,
    pieces,
    gate_part,
    up_part,
    gate_first,
    up_first,
    gate_mid,
    up_mid,
    gate_second,
    up_second,
    left,
    right,
    total,
    gate_sem,
    up_sem,
    down_sem,
    wo_sem,
    near_sem,
    near_send,
    near_recv,
    block_send,
    block_recv,
    swap_send,
    swap_recv,
    att_send,
    att_recv,
    rs_pair_send,
    rs_pair_recv,
    rs_line_send,
    rs_line_recv,
    square_send,
    square_recv,
    ag_line_send,
    ag_line_recv,
    ag_pair_send,
    ag_pair_recv,
    pair_send,
    pair_recv,
    line_send,
    line_recv,
):
    col = lax.axis_index("col")
    row = lax.axis_index("row")
    steps = gate_buf.shape[0]
    wide = gate_buf.shape[2]
    half = wide // 2
    share = gate_part.shape[3]
    _, toks, width = out_ref.shape
    many = cols * share
    spare = wo_ref.shape[0] // wide
    tile = min(512, width)
    col_lines = cols // 2
    pair_me = lax.rem(col, 2)
    line_me = col // 2
    col_other = line_me * 2 + (1 - pair_me)
    row_lines = rows // 2
    core = lax.rem(row, 2)
    depth_me = row // 2
    row_other = depth_me * 2 + (1 - core)

    def line(k):
        return lax.rem(line_me + k, col_lines)

    def layer(k):
        return lax.rem(depth_me + k, row_lines)

    def remote(src, dst, send, recv, axis, device):
        return pltpu.make_async_remote_copy(
            src_ref=src,
            dst_ref=dst,
            send_sem=send,
            recv_sem=recv,
            device_id={axis: device},
            device_id_type=MESH,
        )

    def gate_copy(j):
        return pltpu.make_async_copy(
            gate_ref.at[:, pl.ds(pl.multiple_of(j * wide, wide), wide)], gate_buf.at[j], gate_sem.at[j]
        )

    def up_copy(j):
        return pltpu.make_async_copy(
            up_ref.at[:, pl.ds(pl.multiple_of(j * wide, wide), wide)], up_buf.at[j], up_sem.at[j]
        )

    def down_copy(j):
        return pltpu.make_async_copy(
            down_ref.at[pl.ds(pl.multiple_of(j * wide, wide), wide), :], down_buf.at[j], down_sem.at[j]
        )

    def wo_copy(p):
        return pltpu.make_async_copy(
            wo_ref.at[p * wide : (p + 1) * wide, :], down_buf.at[steps - spare + p], wo_sem.at[p]
        )

    def att_copy(q, k):
        return remote(
            att_ref.at[:, q * toks : (q + 1) * toks, :],
            att_buf.at[q, col],
            att_send.at[q, k - 1],
            att_recv.at[q, k - 1],
            "col",
            lax.rem(col + k, cols),
        )

    def rs_pair(w, q):
        return remote(
            part.at[q, :, 1 - core],
            first.at[q],
            rs_pair_send.at[w, q],
            rs_pair_recv.at[w, q],
            "row",
            row_other,
        )

    def rs_line(w, q, k):
        return remote(
            mid.at[q, layer(k)],
            second.at[q, k - 1],
            rs_line_send.at[w, q, k - 1],
            rs_line_recv.at[w, q, k - 1],
            "row",
            layer(k) * 2 + core,
        )

    def rs_middle(w, q):
        rs_pair(w, q).wait()
        for d in range(row_lines):
            mid[q, d] = (
                part[q, d, core].astype(jnp.float32) + first[q, d].astype(jnp.float32)
            ).astype(jnp.bfloat16)

    def rs_lines_start(w, q):
        for k in range(1, row_lines):
            rs_line(w, q, k).start()

    def rs_finish(w, q):
        result = mid[q, depth_me].astype(jnp.float32)
        for k in range(1, row_lines):
            rs_line(w, q, k).wait()
            result = result + second[q, k - 1].astype(jnp.float32)
        return result

    def square_copy(q, k):
        return remote(
            square_own.at[q],
            square_buf.at[q, k - 1],
            square_send.at[q, k - 1],
            square_recv.at[q, k - 1],
            "col",
            lax.rem(col + k, cols),
        )

    def stream_step(q):
        value = rs_finish(0, q) + res_ref[q].astype(jnp.float32)
        stream[q] = value
        squares = jnp.sum(value * value, axis=1, keepdims=True)
        square_own[q] = jnp.broadcast_to(squares, (toks, 128))
        for k in range(1, cols):
            square_copy(q, k).start()

    def ag_line(q, k):
        return remote(
            pieces.at[q, depth_me, core],
            pieces.at[q, depth_me, core],
            ag_line_send.at[q, k - 1],
            ag_line_recv.at[q, k - 1],
            "row",
            layer(k) * 2 + core,
        )

    def ag_pair(q, k):
        owner = layer(row_lines - k)
        return remote(
            pieces.at[q, owner, core],
            pieces.at[q, owner, core],
            ag_pair_send.at[q, k],
            ag_pair_recv.at[q, k],
            "row",
            row_other,
        )

    def norm_step(q):
        squares = square_own[q]
        for k in range(1, cols):
            square_copy(q, k).wait()
            squares = squares + square_buf[q, k - 1]
        factor = lax.rsqrt(squares / (width * cols) + 1e-05)[:, :1]
        pieces[q, depth_me, core] = (stream[q] * factor * gain_ref[...].astype(jnp.float32)[None, :]).astype(
            jnp.bfloat16
        )
        for k in range(1, row_lines):
            ag_line(q, k).start()
        ag_pair(q, 0).start()

    def ag_forward(q):
        for k in range(1, row_lines):
            ag_line(q, k).wait()
            ag_pair(q, k).start()

    def ag_done(q):
        for k in range(row_lines):
            ag_pair(q, k).wait()

    def transfers(stage, step):
        slot = lax.rem(step, SLOTS)
        hold = lax.rem(step, HOLD)
        if stage == 0:
            pair = (gate_part.at[hold, 1 - pair_me], gate_first.at[slot])
            along = [(up_part.at[hold, line(k)], up_first.at[slot, k - 1]) for k in range(1, col_lines)]
        elif stage == 1:
            pair = (up_mid.at[hold, 1 - pair_me], up_second.at[slot])
            along = [(gate_mid.at[hold, line(k)], gate_second.at[slot, k - 1]) for k in range(1, col_lines)]
        elif stage == 2:
            pair = (left.at[slot, 0, 0], left.at[slot, 0, 1])
            along = [(right.at[slot, 0, 0], right.at[slot, 0, k]) for k in range(1, col_lines)]
        else:
            pair = (right.at[slot, 0], right.at[slot, 1])
            along = [(left.at[slot, 0], left.at[slot, k]) for k in range(1, col_lines)]
        copies = [
            remote(*pair, pair_send.at[stage, slot], pair_recv.at[stage, slot], "col", col_other)
        ]
        for k in range(1, col_lines):
            copies.append(
                remote(
                    *along[k - 1],
                    line_send.at[stage, slot, k - 1],
                    line_recv.at[stage, slot, k - 1],
                    "col",
                    line(k) * 2 + pair_me,
                )
            )
        return copies

    for p in range(spare):
        wo_copy(p).start()

    def begin():
        for j in range(steps):
            gate_copy(j).start()
            up_copy(j).start()
        for j in range(steps - spare):
            down_copy(j).start()

    finish = attention(
        rows,
        cols,
        local_blocks,
        begin,
        query_ref,
        block_ref,
        lists_ref,
        near_key_ref,
        near_value_ref,
        att_ref,
        held,
        near,
        turned,
        top,
        norm,
        acc,
        stats,
        near_sem,
        near_send,
        near_recv,
        block_send,
        block_recv,
        swap_send,
        swap_recv,
    )
    for q in range(NC):
        for k in range(1, cols):
            att_copy(q, k).start()
    total[...] = jnp.zeros_like(total)
    for p in range(spare):
        wo_copy(p).wait()

    def project(q):
        att_buf[q, col] = att_ref[:, q * toks : (q + 1) * toks, :]
        for k in range(1, cols):
            att_copy(q, k).wait()
        inputs = att_buf[q].reshape(many, att_buf.shape[-1])
        for start in range(0, width, tile):
            product = jnp.zeros((many, tile), jnp.float32)
            for p in range(spare):
                product = product + jnp.dot(
                    inputs[:, p * wide : (p + 1) * wide],
                    down_buf[steps - spare + p, :, start : start + tile],
                    preferred_element_type=jnp.float32,
                )
            part[q, :, :, :, start : start + tile] = product.astype(jnp.bfloat16).reshape(
                row_lines, 2, toks, tile
            )
        rs_pair(0, q).start()

    project(0)
    rs_middle(0, 0)
    rs_lines_start(0, 0)
    project(1)
    rs_middle(0, 1)
    rs_lines_start(0, 1)
    stream_step(0)
    norm_step(0)
    stream_step(1)
    norm_step(1)
    for q in range(2, NC):
        project(q)
    for j in range(steps - spare, steps):
        down_copy(j).start()
    for q in range(2, NC):
        rs_middle(0, q)
    ag_forward(0)
    rs_lines_start(0, 2)

    finish()
    chunks = NC * steps

    def stage_when(i, stage):
        return pl.when((i >= LAGS[stage]) & (i < chunks + LAGS[stage]))

    def iteration(i, carry):
        q_now = i // steps
        j_now = lax.rem(i, steps)

        @pl.when((j_now == 0) & (q_now < NC))
        def _():
            ag_done(q_now)

        @stage_when(i, 0)
        def _():
            @pl.when(i < steps)
            def _():
                gate_copy(i).wait()
                up_copy(i).wait()

            hold = lax.rem(i, HOLD)
            inputs = pieces[q_now].reshape(many, pieces.shape[-1])
            product = jnp.dot(inputs, gate_buf[j_now], preferred_element_type=jnp.float32).astype(jnp.bfloat16)
            for b in range(cols):
                gate_part[hold, b % 2, b // 2] = product[b * share : (b + 1) * share]
            product = jnp.dot(inputs, up_buf[j_now], preferred_element_type=jnp.float32).astype(jnp.bfloat16)
            for b in range(cols):
                up_part[hold, b // 2, b % 2] = product[b * share : (b + 1) * share]
            for copy in transfers(0, i):
                copy.start()

        @stage_when(i, 1)
        def _():
            step = i - LAGS[1]
            slot = lax.rem(step, SLOTS)
            hold = lax.rem(step, HOLD)
            for copy in transfers(0, step):
                copy.wait()
            gate_mid[hold] = (
                gate_part[hold, pair_me].astype(jnp.float32) + gate_first[slot].astype(jnp.float32)
            ).astype(jnp.bfloat16)
            up_sum = up_part[hold, line_me].astype(jnp.float32)
            for k in range(1, col_lines):
                up_sum = up_sum + up_first[slot, k - 1].astype(jnp.float32)
            up_mid[hold] = up_sum.astype(jnp.bfloat16)
            for copy in transfers(1, step):
                copy.start()

        @stage_when(i, 2)
        def _():
            step = i - LAGS[2]
            slot = lax.rem(step, SLOTS)
            hold = lax.rem(step, HOLD)
            for copy in transfers(1, step):
                copy.wait()
            gate = gate_mid[hold, line_me].astype(jnp.float32)
            for k in range(1, col_lines):
                gate = gate + gate_second[slot, k - 1].astype(jnp.float32)
            up = up_mid[hold, pair_me].astype(jnp.float32) + up_second[slot].astype(jnp.float32)
            hidden = (gate / (1.0 + jnp.exp(-gate)) * up).astype(jnp.bfloat16)
            left[slot, 0, 0] = hidden[:, :half]
            right[slot, 0, 0] = hidden[:, half:]
            for copy in transfers(2, step):
                copy.start()

        @stage_when(i, 3)
        def _():
            for copy in transfers(2, i - LAGS[3]):
                copy.wait()
            for copy in transfers(3, i - LAGS[3]):
                copy.start()

        @stage_when(i, 4)
        def _():
            step = i - LAGS[4]
            j = lax.rem(step, steps)
            slot = lax.rem(step, SLOTS)

            @pl.when(step < steps)
            def _():
                down_copy(step).wait()

            for copy in transfers(3, step):
                copy.wait()
            gathered = jnp.concatenate(
                [
                    jnp.concatenate([left[slot, k, p], right[slot, p, k]], axis=1)
                    for p in range(2)
                    for k in range(col_lines)
                ],
                axis=0,
            )
            for start in range(0, width, tile):
                total[:, start : start + tile] += jnp.dot(
                    gathered,
                    down_buf[j, :, start : start + tile],
                    preferred_element_type=jnp.float32,
                )

        @pl.when((j_now == 1) & (q_now + 2 < NC))
        def _():
            stream_step(q_now + 2)

        @pl.when((j_now == 2) & (q_now + 2 < NC))
        def _():
            norm_step(q_now + 2)

        @pl.when((j_now == 2) & (q_now + 3 < NC))
        def _():
            rs_lines_start(0, q_now + 3)

        @pl.when((j_now == 4) & (q_now + 1 < NC))
        def _():
            ag_forward(q_now + 1)

        done = i - LAGS[4] + 1
        q_done = done // steps - 1

        @pl.when((done > 0) & (lax.rem(done, steps) == 0))
        def _():
            for p in range(2):
                for k in range(col_lines):
                    owner = line(col_lines - k) * 2 + lax.rem(pair_me + p, 2)
                    begin = (p * col_lines + k) * share
                    part[q_done, owner] = (
                        total[begin : begin + share, :].astype(jnp.bfloat16).reshape(2, toks, width)
                    )
            rs_pair(1, q_done).start()
            total[...] = jnp.zeros_like(total)

        @pl.when((done > steps) & (lax.rem(done, steps) == 1))
        def _():
            rs_middle(1, q_done)
            rs_lines_start(1, q_done)

        @pl.when((done > steps) & (lax.rem(done, steps) == 5))
        def _():
            out_ref[q_done] = stream[q_done] + rs_finish(1, q_done)

        return carry

    lax.fori_loop(0, chunks + LAGS[4], iteration, 0)
    rs_middle(1, NC - 1)
    rs_lines_start(1, NC - 1)
    out_ref[NC - 1] = stream[NC - 1] + rs_finish(1, NC - 1)


def layer_call(
    queries,
    blocks,
    block_lists,
    local_blocks,
    stretch_keys,
    stretch_values,
    out_weight,
    residual,
    norm_gain,
    gate_weight,
    up_weight,
    down_weight,
):
    cols = lax.axis_size("col")
    rows = lax.axis_size("row")
    depth, hidden_width = gate_weight.shape
    tokens, width = residual.shape
    inner = out_weight.shape[0]
    wide = hidden_width // STEPS
    toks = tokens // NC
    share = rows * toks // cols
    col_lines = cols // 2
    row_lines = rows // 2
    devices = rows * cols
    lines = BLK * inner // HEAD_DIM
    assert rows == 2 * cols and inner % wide == 0
    vmem = pl.BlockSpec(memory_space=pltpu.VMEM)
    hbm = pl.BlockSpec(memory_space=pl.ANY)
    dma = pltpu.SemaphoreType.DMA

    def held(*shape):
        return pltpu.VMEM(shape, jnp.bfloat16)

    out = pl.pallas_call(
        functools.partial(layer_kernel, cols, rows, local_blocks),
        out_shape=jax.ShapeDtypeStruct((NC, toks, width), jnp.float32),
        in_specs=[vmem, hbm, vmem, hbm, hbm, hbm, vmem, vmem, hbm, hbm, hbm],
        out_specs=vmem,
        scratch_shapes=[
            held(STEPS, depth, wide),
            held(STEPS, depth, wide),
            held(STEPS, wide, width),
            held(devices, 2, BLK, HEAD_DIM),
            held(cols, 2, BLK, HEAD_DIM),
            held(3, HEAD_DIM, lines),
            pltpu.VMEM((2, 1, lines), jnp.float32),
            pltpu.VMEM((2, 1, lines), jnp.float32),
            pltpu.VMEM((2, HEAD_DIM, lines), jnp.float32),
            pltpu.VMEM((2, 2, lines), jnp.float32),
            held(BLK // tokens, tokens, inner),
            held(NC, cols, 2, toks, inner),
            held(NC, row_lines, 2, toks, width),
            held(NC, row_lines, toks, width),
            held(NC, row_lines, toks, width),
            held(NC, row_lines - 1, toks, width),
            pltpu.VMEM((NC, toks, width), jnp.float32),
            pltpu.VMEM((NC, toks, 128), jnp.float32),
            pltpu.VMEM((NC, cols - 1, toks, 128), jnp.float32),
            held(NC, row_lines, 2, toks, depth),
            held(HOLD, 2, col_lines, share, wide),
            held(HOLD, col_lines, 2, share, wide),
            held(SLOTS, col_lines, share, wide),
            held(SLOTS, col_lines - 1, 2, share, wide),
            held(HOLD, col_lines, share, wide),
            held(HOLD, 2, share, wide),
            held(SLOTS, col_lines - 1, share, wide),
            held(SLOTS, share, wide),
            held(SLOTS, col_lines, 2, share, wide // 2),
            held(SLOTS, 2, col_lines, share, wide // 2),
            pltpu.VMEM((cols * share, width), jnp.float32),
            dma((STEPS,)),
            dma((STEPS,)),
            dma((STEPS,)),
            dma((inner // wide,)),
            dma((2,)),
            dma((cols - 1,)),
            dma((cols - 1,)),
            dma((devices,)),
            dma((devices,)),
            dma((3,)),
            dma((3,)),
            dma((NC, cols - 1)),
            dma((NC, cols - 1)),
            dma((2, NC)),
            dma((2, NC)),
            dma((2, NC, row_lines - 1)),
            dma((2, NC, row_lines - 1)),
            dma((NC, cols - 1)),
            dma((NC, cols - 1)),
            dma((NC, row_lines - 1)),
            dma((NC, row_lines - 1)),
            dma((NC, row_lines)),
            dma((NC, row_lines)),
            dma((4, SLOTS)),
            dma((4, SLOTS)),
            dma((4, SLOTS, col_lines - 1)),
            dma((4, SLOTS, col_lines - 1)),
        ],
        compiler_params=pltpu.CompilerParams(
            collective_id=0, has_side_effects=True, vmem_limit_bytes=67 * 1000 * 1000
        ),
    )(
        queries,
        blocks,
        block_lists,
        stretch_keys,
        stretch_values,
        out_weight,
        residual.reshape(NC, toks, width),
        norm_gain,
        gate_weight,
        up_weight,
        down_weight,
    )
    return out.reshape(tokens, width).astype(jnp.bfloat16)


def local(
    queries,
    cache_keys,
    cache_values,
    stretch_keys,
    stretch_values,
    block_lists,
    out_weight,
    residual,
    norm_gain,
    gate_weight,
    up_weight,
    down_weight,
):
    row_count = lax.axis_size("row")
    col_count = lax.axis_size("col")
    row_index = lax.axis_index("row")
    col_index = lax.axis_index("col")
    device_count = row_count * col_count
    my_index = row_index * col_count + col_index
    local_blocks = cache_keys.shape[1] // BLK
    matched = block_lists // local_blocks == my_index
    block_rows = jnp.sum(jnp.where(matched, block_lists % local_blocks, 0), axis=2)
    blocks = gather_blocks(block_rows, cache_keys, cache_values, device_count)
    return layer_call(
        queries,
        blocks,
        block_lists,
        local_blocks,
        stretch_keys,
        stretch_values,
        out_weight,
        residual,
        norm_gain,
        gate_weight,
        up_weight,
        down_weight,
    )


def solution(mesh):
    in_specs = (
        P("col", "row"),
        P(None, ("row", "col"), None),
        P(None, ("row", "col"), None),
        P(None, "col", None),
        P(None, "col", None),
        P(),
        P("row", "col"),
        P("row", "col"),
        P("col"),
        P("col", "row"),
        P("col", "row"),
        P("row", "col"),
    )
    out_specs = P("row", "col")
    return jax.shard_map(local, mesh=mesh, in_specs=in_specs, out_specs=out_specs, check_vma=False)
```

```python
import functools
import math

import jax
import jax.numpy as jnp
from jax import lax
from jax.experimental import pallas as pl
from jax.experimental.pallas import tpu as pltpu
from jax.sharding import PartitionSpec as P

KV_HEADS = 8
HEAD_DIM = 128
BLK = 128
GROUP = 8
SLOTS = 8
HOLD = 4
LAGS = (0, 2, 4, 6, 8)
MESH = pl.DeviceIdType.MESH
NC = 4
STEPS = 7


def gather_kernel(rows_ref, keys_ref, values_ref, out_ref, key_sem, value_sem):
    groups = keys_ref.shape[0]
    cols = rows_ref.shape[0]
    devices = out_ref.shape[0]

    def copies(d):
        group = d * groups // devices
        positions = pl.ds(pl.multiple_of(rows_ref[d % cols, group] * BLK, BLK), BLK)
        return (
            pltpu.make_async_copy(keys_ref.at[group, positions], out_ref.at[d, 0], key_sem.at[d]),
            pltpu.make_async_copy(values_ref.at[group, positions], out_ref.at[d, 1], value_sem.at[d]),
        )

    for d in range(devices):
        for copy in copies(d):
            copy.start()
    for d in range(devices):
        for copy in copies(d):
            copy.wait()


def gather_blocks(block_rows, cache_keys, cache_values, devices):
    dma = pltpu.SemaphoreType.DMA
    return pl.pallas_call(
        gather_kernel,
        out_shape=jax.ShapeDtypeStruct((devices, 2, BLK, HEAD_DIM), cache_keys.dtype),
        in_specs=[
            pl.BlockSpec(memory_space=pltpu.SMEM),
            pl.BlockSpec(memory_space=pl.ANY),
            pl.BlockSpec(memory_space=pl.ANY),
        ],
        out_specs=pl.BlockSpec(memory_space=pltpu.VMEM),
        scratch_shapes=[dma((devices,)), dma((devices,))],
        compiler_params=pltpu.CompilerParams(vmem_limit_bytes=63 * 1024 * 1024),
    )(block_rows, cache_keys, cache_values)


def flipped(index, bits):
    result = index
    place = 1
    while place <= bits:
        if bits // place % 2:
            result = result + place * (1 - 2 * lax.rem(index // place, 2))
        place *= 2
    return result


def attention(
    rows,
    cols,
    local_blocks,
    begin,
    query_ref,
    block_ref,
    lists_ref,
    near_key_ref,
    near_value_ref,
    out_ref,
    held,
    near,
    turned,
    top,
    norm,
    acc,
    stats,
    near_sem,
    near_send,
    near_recv,
    block_send,
    block_recv,
    swap_send,
    swap_recv,
):
    row = lax.axis_index("row")
    col = lax.axis_index("col")
    devices = rows * cols
    layers = rows // 2
    plane = 2 * cols
    depth = row // 2
    core = lax.rem(row, 2)
    low = layers // 2 - 1
    high = layers // 2
    heads = query_ref.shape[1] // HEAD_DIM
    scaling = 1.0 / math.sqrt(HEAD_DIM)
    lines = heads * BLK
    strip = min(256, lines)

    def is_middle(d):
        return jnp.where((d == low) | (d == high), 1, 0)

    paired = is_middle(depth)
    my_middle = low + depth // high
    mirror_row = (layers - 1 - depth) * 2 + core

    def differing(index, bits, size):
        result = 0
        place = 1
        while place < size:
            one = lax.rem(index // place, 2)
            two = lax.rem(bits // place, 2)
            result = result + place * (one + two - 2 * one * two)
            place *= 2
        return result

    def block_parts(kz, e):
        target_depth = flipped(depth, kz)
        target_core = flipped(core, e // cols)
        target_col = flipped(col, e % cols)
        host = target_depth + is_middle(target_depth) * (my_middle - target_depth)
        block = (target_depth * 2 + target_core) * cols + target_col
        return block, host * 2 + target_core, target_col, kz * plane + e

    def block_copy(kz, e):
        block, host_row, host_col, slot = block_parts(kz, e)
        return pltpu.make_async_remote_copy(
            src_ref=block_ref.at[block],
            dst_ref=held.at[slot],
            send_sem=block_send.at[slot],
            recv_sem=block_recv.at[slot],
            device_id={"row": host_row, "col": host_col},
            device_id_type=MESH,
        )

    def own_block(kz):
        block, _, _, slot = block_parts(kz, 0)
        return pltpu.make_async_copy(block_ref.at[block], held.at[slot], block_recv.at[slot])

    def arrived(slot):
        return pltpu.make_async_copy(block_ref.at[0], held.at[slot], block_recv.at[slot])

    def near_copy(k):
        return pltpu.make_async_remote_copy(
            src_ref=near.at[col],
            dst_ref=near.at[col],
            send_sem=near_send.at[k - 1],
            recv_sem=near_recv.at[k - 1],
            device_id={"col": flipped(col, k)},
            device_id_type=MESH,
        )

    def swap(src, dst, index):
        return pltpu.make_async_remote_copy(
            src_ref=src,
            dst_ref=dst,
            send_sem=swap_send.at[index],
            recv_sem=swap_recv.at[index],
            device_id={"row": mirror_row},
            device_id_type=MESH,
        )

    query_swap = swap(turned.at[0], turned.at[1], 0)
    result_swap = swap(turned.at[1], turned.at[2], 1)
    stats_swap = swap(stats.at[0], stats.at[1], 2)

    group = row * heads // GROUP
    own = (
        pltpu.make_async_copy(near_key_ref.at[group], near.at[col, 0], near_sem.at[0]),
        pltpu.make_async_copy(near_value_ref.at[group], near.at[col, 1], near_sem.at[1]),
    )
    for copy in own:
        copy.start()
    for h in range(heads):
        block = query_ref[:, h * HEAD_DIM : (h + 1) * HEAD_DIM].astype(jnp.float32)
        turned[0, :, h * BLK : (h + 1) * BLK] = jnp.transpose(block).astype(jnp.bfloat16)
    barrier = pltpu.get_barrier_semaphore()
    for k in range(1, devices):
        pl.semaphore_signal(
            barrier,
            inc=1,
            device_id={"row": flipped(row, k // cols), "col": flipped(col, k % cols)},
            device_id_type=MESH,
        )
    pl.semaphore_wait(barrier, devices - 1)

    @pl.when(paired == 1)
    def _():
        query_swap.start()

    for kz in list(range(high, layers)) + list(range(high)):
        for e in range(plane):
            if e:
                block_copy(kz, e).start()
            elif kz == 0:
                own_block(0).start()
            elif kz == layers - 1:

                @pl.when(paired == 1)
                def _():
                    own_block(layers - 1).start()

                @pl.when(paired == 0)
                def _():
                    block_copy(layers - 1, 0).start()
            else:
                block_copy(kz, e).start()
    for copy in own:
        copy.wait()
    for k in range(1, cols):
        near_copy(k).start()
    begin()
    top[1] = jnp.full(top.shape[1:], -1e30, jnp.float32)
    norm[1] = jnp.zeros(norm.shape[1:], jnp.float32)
    acc[1] = jnp.zeros(acc.shape[1:], jnp.float32)
    for k in range(1, cols):
        near_copy(k).wait()

    def weighted(values, weights):
        return lax.dot_general(
            values,
            weights.astype(jnp.bfloat16),
            (((0,), (0,)), ((), ())),
            preferred_element_type=jnp.float32,
        )

    near_keys = near[:, 0].reshape(cols * BLK, HEAD_DIM)
    near_values = near[:, 1].reshape(cols * BLK, HEAD_DIM)
    for begin_at in range(0, lines, strip):
        part = slice(begin_at, begin_at + strip)
        scores = jnp.dot(near_keys, turned[0, :, part], preferred_element_type=jnp.float32) * scaling
        position = lax.broadcasted_iota(jnp.int32, scores.shape, 0)
        token = col * BLK + lax.rem(lax.broadcasted_iota(jnp.int32, scores.shape, 1), BLK)
        allowed = position <= token
        scores = jnp.where(allowed, scores, -1e30)
        new_top = jnp.max(scores, axis=0, keepdims=True)
        weights = jnp.where(allowed, jnp.exp(scores - new_top), 0.0)
        top[0, :, part] = new_top
        norm[0, :, part] = jnp.sum(weights, axis=0, keepdims=True)
        acc[0, :, part] = weighted(near_values, weights)

    batch = 4
    turns = plane // batch

    @pl.when(paired == 1)
    def _():
        query_swap.wait()

    def far_batch(index, carry):
        turn = index // turns
        kz = lax.rem(turn + high, layers)
        first = kz * plane + lax.rem(index, turns) * batch
        shared = paired * (kz // high)
        problem_row = row + shared * (mirror_row - row)
        listed = lists_ref[col, pl.ds(problem_row * heads // GROUP, 1), :]
        source_depth = differing(depth, kz + shared * (layers - 1 - 2 * kz), layers)
        bias = []
        for j in range(batch):
            e = lax.rem(first + j, plane)
            source = (source_depth * 2 + differing(core, e // cols, 2)) * cols + differing(
                col, lax.rem(e, cols), cols
            )
            inside = (listed >= source * local_blocks) & (listed < (source + 1) * local_blocks)
            found = jnp.max(jnp.where(inside, 1.0, 0.0), axis=1, keepdims=True)
            bias.append(jnp.broadcast_to(jnp.where(found > 0.5, 0.0, -1e30), (BLK, strip)))
        bias = jnp.concatenate(bias, axis=0)
        for j in range(batch):
            arrived(first + j).wait()

        keys = held[pl.ds(first, batch), 0].reshape(batch * BLK, HEAD_DIM)
        values = held[pl.ds(first, batch), 1].reshape(batch * BLK, HEAD_DIM)
        parts = [slice(begin_at, begin_at + strip) for begin_at in range(0, lines, strip)]
        tops, norms, accs = [], [], []
        for part in parts:
            scores = jnp.dot(keys, turned[shared, :, part], preferred_element_type=jnp.float32) * scaling + bias
            old_top = top[shared, :, part]
            new_top = jnp.maximum(old_top, jnp.max(scores, axis=0, keepdims=True))
            decay = jnp.exp(old_top - new_top)
            weights = jnp.exp(scores - new_top)
            tops.append(new_top)
            norms.append(norm[shared, :, part] * decay + jnp.sum(weights, axis=0, keepdims=True))
            accs.append(acc[shared, :, part] * decay + weighted(values, weights))
        for n, part in enumerate(parts):
            top[shared, :, part] = tops[n]
            norm[shared, :, part] = norms[n]
            acc[shared, :, part] = accs[n]
        return carry

    lax.fori_loop(0, (layers - high) * turns, far_batch, 0)

    @pl.when(paired == 1)
    def _():
        turned[1] = (acc[1] / norm[1]).astype(jnp.bfloat16)
        stats[0, 0:1, :] = top[1]
        stats[0, 1:2, :] = norm[1]
        stats_swap.start()
        result_swap.start()

    lax.fori_loop((layers - high) * turns, layers * turns, far_batch, 0)

    @pl.when(paired == 1)
    def _():
        stats_swap.wait()
        result_swap.wait()
        other_top = stats[1, 0:1, :]
        own_top = top[0]
        both = jnp.maximum(own_top, other_top)
        own_part = jnp.exp(own_top - both)
        other_part = jnp.exp(other_top - both) * stats[1, 1:2, :]
        norm[0] = norm[0] * own_part + other_part
        acc[0] = acc[0] * own_part + turned[2].astype(jnp.float32) * other_part

    halves = out_ref.shape[1]
    for h in range(heads):
        part = slice(h * BLK, (h + 1) * BLK)
        result = jnp.transpose(acc[0, :, part] / norm[0, :, part]).astype(jnp.bfloat16)
        for p in range(BLK // halves):
            out_ref[p, :, h * HEAD_DIM : (h + 1) * HEAD_DIM] = result[p * halves : (p + 1) * halves]

    def finish():
        for kz in range(layers):
            for e in range(plane):
                if e or kz not in (0, layers - 1):
                    block_copy(kz, e).wait_send()

        @pl.when(paired == 0)
        def _():
            block_copy(layers - 1, 0).wait_send()

    return finish


def layer_kernel(
    cols,
    rows,
    local_blocks,
    query_ref,
    block_ref,
    lists_ref,
    near_key_ref,
    near_value_ref,
    wo_ref,
    res_ref,
    gain_ref,
    gate_ref,
    up_ref,
    down_ref,
    out_ref,
    gate_buf,
    up_buf,
    down_buf,
    held,
    near,
    turned,
    top,
    norm,
    acc,
    stats,
    att_ref,
    att_buf,
    part,
    first,
    mid,
    second,
    stream,
    square_own,
    square_buf,
    factors,
    pieces,
    gate_part,
    up_part,
    gate_first,
    up_first,
    gate_mid,
    up_mid,
    gate_second,
    up_second,
    left,
    right,
    total,
    gate_sem,
    up_sem,
    down_sem,
    wo_sem,
    near_sem,
    near_send,
    near_recv,
    block_send,
    block_recv,
    swap_send,
    swap_recv,
    att_send,
    att_recv,
    rs_pair_send,
    rs_pair_recv,
    rs_line_send,
    rs_line_recv,
    square_send,
    square_recv,
    factor_send,
    factor_recv,
    ag_line_send,
    ag_line_recv,
    ag_pair_send,
    ag_pair_recv,
    pair_send,
    pair_recv,
    line_send,
    line_recv,
):
    col = lax.axis_index("col")
    row = lax.axis_index("row")
    steps = gate_buf.shape[0]
    wide = gate_buf.shape[2]
    half = wide // 2
    share = gate_part.shape[3]
    _, toks, width = out_ref.shape
    many = cols * share
    spare = wo_ref.shape[0] // wide
    tile = min(512, width)
    col_lines = cols // 2
    pair_me = lax.rem(col, 2)
    line_me = col // 2
    col_other = line_me * 2 + (1 - pair_me)
    row_lines = rows // 2
    core = lax.rem(row, 2)
    depth_me = row // 2
    row_other = depth_me * 2 + (1 - core)

    def line(k):
        return lax.rem(line_me + k, col_lines)

    def layer(k):
        return lax.rem(depth_me + k, row_lines)

    def remote(src, dst, send, recv, axis, device):
        return pltpu.make_async_remote_copy(
            src_ref=src,
            dst_ref=dst,
            send_sem=send,
            recv_sem=recv,
            device_id={axis: device},
            device_id_type=MESH,
        )

    def gate_copy(j):
        return pltpu.make_async_copy(
            gate_ref.at[:, pl.ds(pl.multiple_of(j * wide, wide), wide)], gate_buf.at[j], gate_sem.at[j]
        )

    def up_copy(j):
        return pltpu.make_async_copy(
            up_ref.at[:, pl.ds(pl.multiple_of(j * wide, wide), wide)], up_buf.at[j], up_sem.at[j]
        )

    def down_copy(j):
        return pltpu.make_async_copy(
            down_ref.at[pl.ds(pl.multiple_of(j * wide, wide), wide), :], down_buf.at[j], down_sem.at[j]
        )

    def wo_copy(p):
        return pltpu.make_async_copy(
            wo_ref.at[p * wide : (p + 1) * wide, :], down_buf.at[steps - spare + p], wo_sem.at[p]
        )

    def att_copy(q, k):
        return remote(
            att_ref.at[:, q * toks : (q + 1) * toks, :],
            att_buf.at[q, col],
            att_send.at[q, k - 1],
            att_recv.at[q, k - 1],
            "col",
            lax.rem(col + k, cols),
        )

    def rs_pair(w, q):
        return remote(
            part.at[q, :, 1 - core],
            first.at[q],
            rs_pair_send.at[w, q],
            rs_pair_recv.at[w, q],
            "row",
            row_other,
        )

    def rs_line(w, q, k):
        return remote(
            mid.at[q, layer(k)],
            second.at[q, k - 1],
            rs_line_send.at[w, q, k - 1],
            rs_line_recv.at[w, q, k - 1],
            "row",
            layer(k) * 2 + core,
        )

    def rs_middle(w, q):
        rs_pair(w, q).wait()
        for d in range(row_lines):
            mid[q, d] = (
                part[q, d, core].astype(jnp.float32) + first[q, d].astype(jnp.float32)
            ).astype(jnp.bfloat16)

    def rs_lines_start(w, q):
        for k in range(1, row_lines):
            rs_line(w, q, k).start()

    def rs_finish(w, q):
        result = mid[q, depth_me].astype(jnp.float32)
        for k in range(1, row_lines):
            rs_line(w, q, k).wait()
            result = result + second[q, k - 1].astype(jnp.float32)
        return result

    def square_copy(q, k):
        return remote(
            square_own.at[q],
            square_buf.at[q, k - 1],
            square_send.at[q, k - 1],
            square_recv.at[q, k - 1],
            "col",
            lax.rem(col + k, cols),
        )

    def stream_step(q):
        value = rs_finish(0, q) + res_ref[q].astype(jnp.float32)
        stream[q] = value
        squares = jnp.sum(value * value, axis=1, keepdims=True)
        square_own[q] = jnp.broadcast_to(squares, (toks, 128))
        for k in range(1, cols):
            square_copy(q, k).start()
        pieces[q, depth_me, core] = (value * gain_ref[...].astype(jnp.float32)[None, :]).astype(jnp.bfloat16)
        for k in range(1, row_lines):
            ag_line(q, k).start()
        ag_pair(q, 0).start()

    def ag_line(q, k):
        return remote(
            pieces.at[q, depth_me, core],
            pieces.at[q, depth_me, core],
            ag_line_send.at[q, k - 1],
            ag_line_recv.at[q, k - 1],
            "row",
            layer(k) * 2 + core,
        )

    def ag_pair(q, k):
        owner = layer(row_lines - k)
        return remote(
            pieces.at[q, owner, core],
            pieces.at[q, owner, core],
            ag_pair_send.at[q, k],
            ag_pair_recv.at[q, k],
            "row",
            row_other,
        )

    def factor_copy(q, k):
        return remote(
            factors.at[q, core],
            factors.at[q, core],
            factor_send.at[q, k - 1],
            factor_recv.at[q, core],
            "row",
            flipped(row, k),
        )

    def factor_step(q):
        squares = square_own[q]
        for k in range(1, cols):
            square_copy(q, k).wait()
            squares = squares + square_buf[q, k - 1]

        @pl.when(depth_me == col)
        def _():
            factors[q, core] = lax.rsqrt(squares / (width * cols) + 1e-05)
            for k in range(1, rows):
                factor_copy(q, k).start()

    def factor_wait(q):
        for c in range(2):

            @pl.when(row != 2 * col + c)
            def _():
                pltpu.make_async_copy(factors.at[q, c], factors.at[q, c], factor_recv.at[q, c]).wait()

    def factor_finish():
        @pl.when(depth_me == col)
        def _():
            for q in range(NC):
                for k in range(1, rows):
                    factor_copy(q, k).wait_send()

    def ag_forward(q):
        for k in range(1, row_lines):
            ag_line(q, k).wait()
            ag_pair(q, k).start()

    def ag_done(q):
        for k in range(row_lines):
            ag_pair(q, k).wait()

    def transfers(stage, step):
        slot = lax.rem(step, SLOTS)
        hold = lax.rem(step, HOLD)
        if stage == 0:
            pair = (gate_part.at[hold, 1 - pair_me], gate_first.at[slot])
            along = [(up_part.at[hold, line(k)], up_first.at[slot, k - 1]) for k in range(1, col_lines)]
        elif stage == 1:
            pair = (up_mid.at[hold, 1 - pair_me], up_second.at[slot])
            along = [(gate_mid.at[hold, line(k)], gate_second.at[slot, k - 1]) for k in range(1, col_lines)]
        elif stage == 2:
            pair = (left.at[slot, 0, 0], left.at[slot, 0, 1])
            along = [(right.at[slot, 0, 0], right.at[slot, 0, k]) for k in range(1, col_lines)]
        else:
            pair = (right.at[slot, 0], right.at[slot, 1])
            along = [(left.at[slot, 0], left.at[slot, k]) for k in range(1, col_lines)]
        copies = [
            remote(*pair, pair_send.at[stage, slot], pair_recv.at[stage, slot], "col", col_other)
        ]
        for k in range(1, col_lines):
            copies.append(
                remote(
                    *along[k - 1],
                    line_send.at[stage, slot, k - 1],
                    line_recv.at[stage, slot, k - 1],
                    "col",
                    line(k) * 2 + pair_me,
                )
            )
        return copies

    for p in range(spare):
        wo_copy(p).start()

    def begin():
        for j in range(steps):
            gate_copy(j).start()
            up_copy(j).start()
        for j in range(steps - spare):
            down_copy(j).start()

    finish = attention(
        rows,
        cols,
        local_blocks,
        begin,
        query_ref,
        block_ref,
        lists_ref,
        near_key_ref,
        near_value_ref,
        att_ref,
        held,
        near,
        turned,
        top,
        norm,
        acc,
        stats,
        near_sem,
        near_send,
        near_recv,
        block_send,
        block_recv,
        swap_send,
        swap_recv,
    )
    for q in range(NC):
        for k in range(1, cols):
            att_copy(q, k).start()
    total[...] = jnp.zeros_like(total)
    for p in range(spare):
        wo_copy(p).wait()

    def project(q):
        att_buf[q, col] = att_ref[:, q * toks : (q + 1) * toks, :]
        for k in range(1, cols):
            att_copy(q, k).wait()
        inputs = att_buf[q].reshape(many, att_buf.shape[-1])
        for start in range(0, width, tile):
            product = jnp.zeros((many, tile), jnp.float32)
            for p in range(spare):
                product = product + jnp.dot(
                    inputs[:, p * wide : (p + 1) * wide],
                    down_buf[steps - spare + p, :, start : start + tile],
                    preferred_element_type=jnp.float32,
                )
            part[q, :, :, :, start : start + tile] = product.astype(jnp.bfloat16).reshape(
                row_lines, 2, toks, tile
            )
        rs_pair(0, q).start()

    project(0)
    rs_middle(0, 0)
    rs_lines_start(0, 0)
    project(1)
    rs_middle(0, 1)
    rs_lines_start(0, 1)
    stream_step(0)
    stream_step(1)
    factor_step(0)
    for q in range(2, NC):
        project(q)
    for j in range(steps - spare, steps):
        down_copy(j).start()
    for q in range(2, NC):
        rs_middle(0, q)
    factor_step(1)
    ag_forward(0)
    rs_lines_start(0, 2)

    finish()
    chunks = NC * steps

    def stage_when(i, stage):
        return pl.when((i >= LAGS[stage]) & (i < chunks + LAGS[stage]))

    def iteration(i, carry):
        q_now = i // steps
        j_now = lax.rem(i, steps)

        @pl.when((j_now == 0) & (q_now < NC))
        def _():
            ag_done(q_now)

        @stage_when(i, 0)
        def _():
            @pl.when(i < steps)
            def _():
                gate_copy(i).wait()
                up_copy(i).wait()

            hold = lax.rem(i, HOLD)
            inputs = pieces[q_now].reshape(many, pieces.shape[-1])
            product = jnp.dot(inputs, gate_buf[j_now], preferred_element_type=jnp.float32).astype(jnp.bfloat16)
            for b in range(cols):
                gate_part[hold, b % 2, b // 2] = product[b * share : (b + 1) * share]
            product = jnp.dot(inputs, up_buf[j_now], preferred_element_type=jnp.float32).astype(jnp.bfloat16)
            for b in range(cols):
                up_part[hold, b // 2, b % 2] = product[b * share : (b + 1) * share]
            for copy in transfers(0, i):
                copy.start()

        @stage_when(i, 1)
        def _():
            step = i - LAGS[1]
            slot = lax.rem(step, SLOTS)
            hold = lax.rem(step, HOLD)
            for copy in transfers(0, step):
                copy.wait()
            gate_mid[hold] = (
                gate_part[hold, pair_me].astype(jnp.float32) + gate_first[slot].astype(jnp.float32)
            ).astype(jnp.bfloat16)
            up_sum = up_part[hold, line_me].astype(jnp.float32)
            for k in range(1, col_lines):
                up_sum = up_sum + up_first[slot, k - 1].astype(jnp.float32)
            up_mid[hold] = up_sum.astype(jnp.bfloat16)
            for copy in transfers(1, step):
                copy.start()

        @stage_when(i, 2)
        def _():
            step = i - LAGS[2]
            slot = lax.rem(step, SLOTS)
            hold = lax.rem(step, HOLD)
            for copy in transfers(1, step):
                copy.wait()
            gate = gate_mid[hold, line_me].astype(jnp.float32)
            for k in range(1, col_lines):
                gate = gate + gate_second[slot, k - 1].astype(jnp.float32)
            up = up_mid[hold, pair_me].astype(jnp.float32) + up_second[slot].astype(jnp.float32)
            q = step // steps

            @pl.when(lax.rem(step, steps) == 0)
            def _():
                factor_wait(q)

            factor = factors[q].reshape(share, 128)[:, :1]
            gate = gate * factor
            hidden = (gate / (1.0 + jnp.exp(-gate)) * (up * factor)).astype(jnp.bfloat16)
            left[slot, 0, 0] = hidden[:, :half]
            right[slot, 0, 0] = hidden[:, half:]
            for copy in transfers(2, step):
                copy.start()

        @stage_when(i, 3)
        def _():
            for copy in transfers(2, i - LAGS[3]):
                copy.wait()
            for copy in transfers(3, i - LAGS[3]):
                copy.start()

        @stage_when(i, 4)
        def _():
            step = i - LAGS[4]
            j = lax.rem(step, steps)
            slot = lax.rem(step, SLOTS)

            @pl.when(step < steps)
            def _():
                down_copy(step).wait()

            for copy in transfers(3, step):
                copy.wait()
            gathered = jnp.concatenate(
                [
                    jnp.concatenate([left[slot, k, p], right[slot, p, k]], axis=1)
                    for p in range(2)
                    for k in range(col_lines)
                ],
                axis=0,
            )
            for start in range(0, width, tile):
                total[:, start : start + tile] += jnp.dot(
                    gathered,
                    down_buf[j, :, start : start + tile],
                    preferred_element_type=jnp.float32,
                )

        @pl.when((j_now == 5) & (q_now + 2 < NC))
        def _():
            stream_step(q_now + 2)

        @pl.when((j_now == 6) & (q_now + 2 < NC))
        def _():
            factor_step(q_now + 2)

        @pl.when((j_now == 5) & (q_now + 3 < NC))
        def _():
            rs_lines_start(0, q_now + 3)

        @pl.when((j_now == 5) & (q_now + 1 < NC))
        def _():
            ag_forward(q_now + 1)

        done = i - LAGS[4] + 1
        q_done = done // steps - 1

        @pl.when((done > 0) & (lax.rem(done, steps) == 0))
        def _():
            for p in range(2):
                for k in range(col_lines):
                    owner = line(col_lines - k) * 2 + lax.rem(pair_me + p, 2)
                    begin = (p * col_lines + k) * share
                    part[q_done, owner] = (
                        total[begin : begin + share, :].astype(jnp.bfloat16).reshape(2, toks, width)
                    )
            rs_pair(1, q_done).start()
            total[...] = jnp.zeros_like(total)

        @pl.when((done > steps) & (lax.rem(done, steps) == 1))
        def _():
            rs_middle(1, q_done)
            rs_lines_start(1, q_done)

        @pl.when((done > steps) & (lax.rem(done, steps) == 5))
        def _():
            out_ref[q_done] = stream[q_done] + rs_finish(1, q_done)

        return carry

    lax.fori_loop(0, chunks + LAGS[4], iteration, 0)
    factor_finish()
    rs_middle(1, NC - 1)
    rs_lines_start(1, NC - 1)
    out_ref[NC - 1] = stream[NC - 1] + rs_finish(1, NC - 1)


def layer_call(
    queries,
    blocks,
    block_lists,
    local_blocks,
    stretch_keys,
    stretch_values,
    out_weight,
    residual,
    norm_gain,
    gate_weight,
    up_weight,
    down_weight,
):
    cols = lax.axis_size("col")
    rows = lax.axis_size("row")
    depth, hidden_width = gate_weight.shape
    tokens, width = residual.shape
    inner = out_weight.shape[0]
    wide = hidden_width // STEPS
    toks = tokens // NC
    share = rows * toks // cols
    col_lines = cols // 2
    row_lines = rows // 2
    devices = rows * cols
    lines = BLK * inner // HEAD_DIM
    assert rows == 2 * cols and inner % wide == 0
    vmem = pl.BlockSpec(memory_space=pltpu.VMEM)
    hbm = pl.BlockSpec(memory_space=pl.ANY)
    dma = pltpu.SemaphoreType.DMA

    def held(*shape):
        return pltpu.VMEM(shape, jnp.bfloat16)

    out = pl.pallas_call(
        functools.partial(layer_kernel, cols, rows, local_blocks),
        out_shape=jax.ShapeDtypeStruct((NC, toks, width), jnp.float32),
        in_specs=[vmem, hbm, vmem, hbm, hbm, hbm, vmem, vmem, hbm, hbm, hbm],
        out_specs=vmem,
        scratch_shapes=[
            held(STEPS, depth, wide),
            held(STEPS, depth, wide),
            held(STEPS, wide, width),
            held(devices, 2, BLK, HEAD_DIM),
            held(cols, 2, BLK, HEAD_DIM),
            held(3, HEAD_DIM, lines),
            pltpu.VMEM((2, 1, lines), jnp.float32),
            pltpu.VMEM((2, 1, lines), jnp.float32),
            pltpu.VMEM((2, HEAD_DIM, lines), jnp.float32),
            pltpu.VMEM((2, 2, lines), jnp.float32),
            held(BLK // tokens, tokens, inner),
            held(NC, cols, 2, toks, inner),
            held(NC, row_lines, 2, toks, width),
            held(NC, row_lines, toks, width),
            held(NC, row_lines, toks, width),
            held(NC, row_lines - 1, toks, width),
            pltpu.VMEM((NC, toks, width), jnp.float32),
            pltpu.VMEM((NC, toks, 128), jnp.float32),
            pltpu.VMEM((NC, cols - 1, toks, 128), jnp.float32),
            pltpu.VMEM((NC, 2, toks, 128), jnp.float32),
            held(NC, row_lines, 2, toks, depth),
            held(HOLD, 2, col_lines, share, wide),
            held(HOLD, col_lines, 2, share, wide),
            held(SLOTS, col_lines, share, wide),
            held(SLOTS, col_lines - 1, 2, share, wide),
            held(HOLD, col_lines, share, wide),
            held(HOLD, 2, share, wide),
            held(SLOTS, col_lines - 1, share, wide),
            held(SLOTS, share, wide),
            held(SLOTS, col_lines, 2, share, wide // 2),
            held(SLOTS, 2, col_lines, share, wide // 2),
            pltpu.VMEM((cols * share, width), jnp.float32),
            dma((STEPS,)),
            dma((STEPS,)),
            dma((STEPS,)),
            dma((inner // wide,)),
            dma((2,)),
            dma((cols - 1,)),
            dma((cols - 1,)),
            dma((devices,)),
            dma((devices,)),
            dma((3,)),
            dma((3,)),
            dma((NC, cols - 1)),
            dma((NC, cols - 1)),
            dma((2, NC)),
            dma((2, NC)),
            dma((2, NC, row_lines - 1)),
            dma((2, NC, row_lines - 1)),
            dma((NC, cols - 1)),
            dma((NC, cols - 1)),
            dma((NC, rows - 1)),
            dma((NC, 2)),
            dma((NC, row_lines - 1)),
            dma((NC, row_lines - 1)),
            dma((NC, row_lines)),
            dma((NC, row_lines)),
            dma((4, SLOTS)),
            dma((4, SLOTS)),
            dma((4, SLOTS, col_lines - 1)),
            dma((4, SLOTS, col_lines - 1)),
        ],
        compiler_params=pltpu.CompilerParams(
            collective_id=0, has_side_effects=True, vmem_limit_bytes=67 * 1000 * 1000
        ),
    )(
        queries,
        blocks,
        block_lists,
        stretch_keys,
        stretch_values,
        out_weight,
        residual.reshape(NC, toks, width),
        norm_gain,
        gate_weight,
        up_weight,
        down_weight,
    )
    return out.reshape(tokens, width).astype(jnp.bfloat16)


def local(
    queries,
    cache_keys,
    cache_values,
    stretch_keys,
    stretch_values,
    block_lists,
    out_weight,
    residual,
    norm_gain,
    gate_weight,
    up_weight,
    down_weight,
):
    row_count = lax.axis_size("row")
    col_count = lax.axis_size("col")
    row_index = lax.axis_index("row")
    col_index = lax.axis_index("col")
    device_count = row_count * col_count
    my_index = row_index * col_count + col_index
    local_blocks = cache_keys.shape[1] // BLK
    matched = block_lists // local_blocks == my_index
    block_rows = jnp.sum(jnp.where(matched, block_lists % local_blocks, 0), axis=2)
    blocks = gather_blocks(block_rows, cache_keys, cache_values, device_count)
    return layer_call(
        queries,
        blocks,
        block_lists,
        local_blocks,
        stretch_keys,
        stretch_values,
        out_weight,
        residual,
        norm_gain,
        gate_weight,
        up_weight,
        down_weight,
    )


def solution(mesh):
    in_specs = (
        P("col", "row"),
        P(None, ("row", "col"), None),
        P(None, ("row", "col"), None),
        P(None, "col", None),
        P(None, "col", None),
        P(),
        P("row", "col"),
        P("row", "col"),
        P("col"),
        P("col", "row"),
        P("col", "row"),
        P("row", "col"),
    )
    out_specs = P("row", "col")
    return jax.shard_map(local, mesh=mesh, in_specs=in_specs, out_specs=out_specs, check_vma=False)
```

```python
import functools
import math

import jax
import jax.numpy as jnp
from jax import lax
from jax.experimental import pallas as pl
from jax.experimental.pallas import tpu as pltpu
from jax.sharding import PartitionSpec as P

KV_HEADS = 8
HEAD_DIM = 128
BLK = 128
GROUP = 8
SLOTS = 8
HOLD = 4
LAGS = (0, 2, 4, 6, 8)
MESH = pl.DeviceIdType.MESH
NC = 4
STEPS = 7


def gather_kernel(rows_ref, keys_ref, values_ref, out_ref, key_sem, value_sem):
    groups = keys_ref.shape[0]
    cols = rows_ref.shape[0]
    devices = out_ref.shape[0]

    def copies(d):
        group = d * groups // devices
        positions = pl.ds(pl.multiple_of(rows_ref[d % cols, group] * BLK, BLK), BLK)
        return (
            pltpu.make_async_copy(keys_ref.at[group, positions], out_ref.at[d, 0], key_sem.at[d]),
            pltpu.make_async_copy(values_ref.at[group, positions], out_ref.at[d, 1], value_sem.at[d]),
        )

    for d in range(devices):
        for copy in copies(d):
            copy.start()
    for d in range(devices):
        for copy in copies(d):
            copy.wait()


def gather_blocks(block_rows, cache_keys, cache_values, devices):
    dma = pltpu.SemaphoreType.DMA
    return pl.pallas_call(
        gather_kernel,
        out_shape=jax.ShapeDtypeStruct((devices, 2, BLK, HEAD_DIM), cache_keys.dtype),
        in_specs=[
            pl.BlockSpec(memory_space=pltpu.SMEM),
            pl.BlockSpec(memory_space=pl.ANY),
            pl.BlockSpec(memory_space=pl.ANY),
        ],
        out_specs=pl.BlockSpec(memory_space=pltpu.VMEM),
        scratch_shapes=[dma((devices,)), dma((devices,))],
        compiler_params=pltpu.CompilerParams(vmem_limit_bytes=63 * 1024 * 1024),
    )(block_rows, cache_keys, cache_values)


def flipped(index, bits):
    result = index
    place = 1
    while place <= bits:
        if bits // place % 2:
            result = result + place * (1 - 2 * lax.rem(index // place, 2))
        place *= 2
    return result


def attention(
    rows,
    cols,
    local_blocks,
    begin,
    query_ref,
    block_ref,
    lists_ref,
    near_key_ref,
    near_value_ref,
    out_ref,
    held,
    near,
    turned,
    top,
    norm,
    acc,
    stats,
    near_sem,
    near_send,
    near_recv,
    block_send,
    block_recv,
    swap_send,
    swap_recv,
):
    row = lax.axis_index("row")
    col = lax.axis_index("col")
    devices = rows * cols
    layers = rows // 2
    plane = 2 * cols
    depth = row // 2
    core = lax.rem(row, 2)
    low = layers // 2 - 1
    high = layers // 2
    heads = query_ref.shape[1] // HEAD_DIM
    scaling = 1.0 / math.sqrt(HEAD_DIM)
    lines = heads * BLK
    strip = min(256, lines)

    def is_middle(d):
        return jnp.where((d == low) | (d == high), 1, 0)

    paired = is_middle(depth)
    my_middle = low + depth // high
    mirror_row = (layers - 1 - depth) * 2 + core

    def differing(index, bits, size):
        result = 0
        place = 1
        while place < size:
            one = lax.rem(index // place, 2)
            two = lax.rem(bits // place, 2)
            result = result + place * (one + two - 2 * one * two)
            place *= 2
        return result

    def block_parts(kz, e):
        target_depth = flipped(depth, kz)
        target_core = flipped(core, e // cols)
        target_col = flipped(col, e % cols)
        host = target_depth + is_middle(target_depth) * (my_middle - target_depth)
        block = (target_depth * 2 + target_core) * cols + target_col
        return block, host * 2 + target_core, target_col, kz * plane + e

    def block_copy(kz, e):
        block, host_row, host_col, slot = block_parts(kz, e)
        return pltpu.make_async_remote_copy(
            src_ref=block_ref.at[block],
            dst_ref=held.at[slot],
            send_sem=block_send.at[slot],
            recv_sem=block_recv.at[slot],
            device_id={"row": host_row, "col": host_col},
            device_id_type=MESH,
        )

    def own_block(kz):
        block, _, _, slot = block_parts(kz, 0)
        return pltpu.make_async_copy(block_ref.at[block], held.at[slot], block_recv.at[slot])

    def arrived(slot):
        return pltpu.make_async_copy(block_ref.at[0], held.at[slot], block_recv.at[slot])

    def near_copy(k):
        return pltpu.make_async_remote_copy(
            src_ref=near.at[col],
            dst_ref=near.at[col],
            send_sem=near_send.at[k - 1],
            recv_sem=near_recv.at[k - 1],
            device_id={"col": flipped(col, k)},
            device_id_type=MESH,
        )

    def swap(src, dst, index):
        return pltpu.make_async_remote_copy(
            src_ref=src,
            dst_ref=dst,
            send_sem=swap_send.at[index],
            recv_sem=swap_recv.at[index],
            device_id={"row": mirror_row},
            device_id_type=MESH,
        )

    query_swap = swap(turned.at[0], turned.at[1], 0)
    result_swap = swap(turned.at[1], turned.at[2], 1)
    stats_swap = swap(stats.at[0], stats.at[1], 2)

    group = row * heads // GROUP
    own = (
        pltpu.make_async_copy(near_key_ref.at[group], near.at[col, 0], near_sem.at[0]),
        pltpu.make_async_copy(near_value_ref.at[group], near.at[col, 1], near_sem.at[1]),
    )
    for copy in own:
        copy.start()
    for h in range(heads):
        block = query_ref[:, h * HEAD_DIM : (h + 1) * HEAD_DIM].astype(jnp.float32)
        turned[0, :, h * BLK : (h + 1) * BLK] = jnp.transpose(block).astype(jnp.bfloat16)
    barrier = pltpu.get_barrier_semaphore()
    for k in range(1, devices):
        pl.semaphore_signal(
            barrier,
            inc=1,
            device_id={"row": flipped(row, k // cols), "col": flipped(col, k % cols)},
            device_id_type=MESH,
        )
    pl.semaphore_wait(barrier, devices - 1)

    @pl.when(paired == 1)
    def _():
        query_swap.start()

    for kz in list(range(high, layers)) + list(range(high)):
        for e in range(plane):
            if e:
                block_copy(kz, e).start()
            elif kz == 0:
                own_block(0).start()
            elif kz == layers - 1:

                @pl.when(paired == 1)
                def _():
                    own_block(layers - 1).start()

                @pl.when(paired == 0)
                def _():
                    block_copy(layers - 1, 0).start()
            else:
                block_copy(kz, e).start()
    for copy in own:
        copy.wait()
    for k in range(1, cols):
        near_copy(k).start()
    begin()
    top[1] = jnp.full(top.shape[1:], -1e30, jnp.float32)
    norm[1] = jnp.zeros(norm.shape[1:], jnp.float32)
    acc[1] = jnp.zeros(acc.shape[1:], jnp.float32)
    for k in range(1, cols):
        near_copy(k).wait()

    def weighted(values, weights):
        return lax.dot_general(
            values,
            weights.astype(jnp.bfloat16),
            (((0,), (0,)), ((), ())),
            preferred_element_type=jnp.float32,
        )

    near_keys = near[:, 0].reshape(cols * BLK, HEAD_DIM)
    near_values = near[:, 1].reshape(cols * BLK, HEAD_DIM)
    for begin_at in range(0, lines, strip):
        part = slice(begin_at, begin_at + strip)
        scores = jnp.dot(near_keys, turned[0, :, part], preferred_element_type=jnp.float32) * scaling
        position = lax.broadcasted_iota(jnp.int32, scores.shape, 0)
        token = col * BLK + lax.rem(lax.broadcasted_iota(jnp.int32, scores.shape, 1), BLK)
        allowed = position <= token
        scores = jnp.where(allowed, scores, -1e30)
        new_top = jnp.max(scores, axis=0, keepdims=True)
        weights = jnp.where(allowed, jnp.exp(scores - new_top), 0.0)
        top[0, :, part] = new_top
        norm[0, :, part] = jnp.sum(weights, axis=0, keepdims=True)
        acc[0, :, part] = weighted(near_values, weights)

    batch = 4
    turns = plane // batch

    @pl.when(paired == 1)
    def _():
        query_swap.wait()

    def far_batch(index, carry):
        turn = index // turns
        kz = lax.rem(turn + high, layers)
        first = kz * plane + lax.rem(index, turns) * batch
        shared = paired * (kz // high)
        problem_row = row + shared * (mirror_row - row)
        listed = lists_ref[col, pl.ds(problem_row * heads // GROUP, 1), :]
        source_depth = differing(depth, kz + shared * (layers - 1 - 2 * kz), layers)
        bias = []
        for j in range(batch):
            e = lax.rem(first + j, plane)
            source = (source_depth * 2 + differing(core, e // cols, 2)) * cols + differing(
                col, lax.rem(e, cols), cols
            )
            inside = (listed >= source * local_blocks) & (listed < (source + 1) * local_blocks)
            found = jnp.max(jnp.where(inside, 1.0, 0.0), axis=1, keepdims=True)
            bias.append(jnp.broadcast_to(jnp.where(found > 0.5, 0.0, -1e30), (BLK, strip)))
        bias = jnp.concatenate(bias, axis=0)
        for j in range(batch):
            arrived(first + j).wait()

        keys = held[pl.ds(first, batch), 0].reshape(batch * BLK, HEAD_DIM)
        values = held[pl.ds(first, batch), 1].reshape(batch * BLK, HEAD_DIM)
        parts = [slice(begin_at, begin_at + strip) for begin_at in range(0, lines, strip)]
        tops, norms, accs = [], [], []
        for part in parts:
            scores = jnp.dot(keys, turned[shared, :, part], preferred_element_type=jnp.float32) * scaling + bias
            old_top = top[shared, :, part]
            new_top = jnp.maximum(old_top, jnp.max(scores, axis=0, keepdims=True))
            decay = jnp.exp(old_top - new_top)
            weights = jnp.exp(scores - new_top)
            tops.append(new_top)
            norms.append(norm[shared, :, part] * decay + jnp.sum(weights, axis=0, keepdims=True))
            accs.append(acc[shared, :, part] * decay + weighted(values, weights))
        for n, part in enumerate(parts):
            top[shared, :, part] = tops[n]
            norm[shared, :, part] = norms[n]
            acc[shared, :, part] = accs[n]
        return carry

    lax.fori_loop(0, (layers - high) * turns, far_batch, 0)

    @pl.when(paired == 1)
    def _():
        turned[1] = (acc[1] / norm[1]).astype(jnp.bfloat16)
        stats[0, 0:1, :] = top[1]
        stats[0, 1:2, :] = norm[1]
        stats_swap.start()
        result_swap.start()

    lax.fori_loop((layers - high) * turns, layers * turns, far_batch, 0)

    @pl.when(paired == 1)
    def _():
        stats_swap.wait()
        result_swap.wait()
        other_top = stats[1, 0:1, :]
        own_top = top[0]
        both = jnp.maximum(own_top, other_top)
        own_part = jnp.exp(own_top - both)
        other_part = jnp.exp(other_top - both) * stats[1, 1:2, :]
        norm[0] = norm[0] * own_part + other_part
        acc[0] = acc[0] * own_part + turned[2].astype(jnp.float32) * other_part

    halves = out_ref.shape[1]
    for h in range(heads):
        part = slice(h * BLK, (h + 1) * BLK)
        result = jnp.transpose(acc[0, :, part] / norm[0, :, part]).astype(jnp.bfloat16)
        for p in range(BLK // halves):
            out_ref[p, :, h * HEAD_DIM : (h + 1) * HEAD_DIM] = result[p * halves : (p + 1) * halves]

    def finish():
        for kz in range(layers):
            for e in range(plane):
                if e or kz not in (0, layers - 1):
                    block_copy(kz, e).wait_send()

        @pl.when(paired == 0)
        def _():
            block_copy(layers - 1, 0).wait_send()

    return finish


def layer_kernel(
    cols,
    rows,
    local_blocks,
    query_ref,
    block_ref,
    lists_ref,
    near_key_ref,
    near_value_ref,
    wo_ref,
    res_ref,
    gain_ref,
    gate_ref,
    up_ref,
    down_ref,
    out_ref,
    gate_buf,
    up_buf,
    down_buf,
    held,
    near,
    turned,
    top,
    norm,
    acc,
    stats,
    att_ref,
    att_buf,
    part,
    first,
    mid,
    second,
    stream,
    square_own,
    square_buf,
    factors,
    pieces,
    gate_part,
    up_part,
    gate_first,
    up_first,
    gate_mid,
    up_mid,
    gate_second,
    up_second,
    left,
    right,
    total,
    gate_sem,
    up_sem,
    down_sem,
    wo_sem,
    near_sem,
    near_send,
    near_recv,
    block_send,
    block_recv,
    swap_send,
    swap_recv,
    att_send,
    att_recv,
    rs_pair_send,
    rs_pair_recv,
    rs_line_send,
    rs_line_recv,
    square_send,
    square_recv,
    factor_send,
    factor_recv,
    ag_line_send,
    ag_line_recv,
    ag_pair_send,
    ag_pair_recv,
    pair_send,
    pair_recv,
    line_send,
    line_recv,
):
    col = lax.axis_index("col")
    row = lax.axis_index("row")
    steps = gate_buf.shape[0]
    wide = gate_buf.shape[2]
    half = wide // 2
    share = gate_part.shape[3]
    _, toks, width = out_ref.shape
    many = cols * share
    spare = wo_ref.shape[0] // wide
    tile = min(512, width)
    col_lines = cols // 2
    pair_me = lax.rem(col, 2)
    line_me = col // 2
    col_other = line_me * 2 + (1 - pair_me)
    row_lines = rows // 2
    core = lax.rem(row, 2)
    depth_me = row // 2
    row_other = depth_me * 2 + (1 - core)

    def line(k):
        return lax.rem(line_me + k, col_lines)

    def layer(k):
        return lax.rem(depth_me + k, row_lines)

    def remote(src, dst, send, recv, axis, device):
        return pltpu.make_async_remote_copy(
            src_ref=src,
            dst_ref=dst,
            send_sem=send,
            recv_sem=recv,
            device_id={axis: device},
            device_id_type=MESH,
        )

    def gate_copy(j):
        return pltpu.make_async_copy(
            gate_ref.at[:, pl.ds(pl.multiple_of(j * wide, wide), wide)], gate_buf.at[j], gate_sem.at[j]
        )

    def up_copy(j):
        return pltpu.make_async_copy(
            up_ref.at[:, pl.ds(pl.multiple_of(j * wide, wide), wide)], up_buf.at[j], up_sem.at[j]
        )

    def down_copy(j):
        return pltpu.make_async_copy(
            down_ref.at[pl.ds(pl.multiple_of(j * wide, wide), wide), :], down_buf.at[j], down_sem.at[j]
        )

    def wo_copy(p):
        return pltpu.make_async_copy(
            wo_ref.at[p * wide : (p + 1) * wide, :], down_buf.at[steps - spare + p], wo_sem.at[p]
        )

    def att_copy(q, k):
        return remote(
            att_ref.at[:, q * toks : (q + 1) * toks, :],
            att_buf.at[q, col],
            att_send.at[q, k - 1],
            att_recv.at[q, k - 1],
            "col",
            lax.rem(col + k, cols),
        )

    def rs_pair(w, q):
        return remote(
            part.at[q, :, 1 - core],
            first.at[q],
            rs_pair_send.at[w, q],
            rs_pair_recv.at[w, q],
            "row",
            row_other,
        )

    def rs_line(w, q, k):
        return remote(
            mid.at[q, layer(k)],
            second.at[q, k - 1],
            rs_line_send.at[w, q, k - 1],
            rs_line_recv.at[w, q, k - 1],
            "row",
            layer(k) * 2 + core,
        )

    def rs_middle(w, q):
        rs_pair(w, q).wait()
        for d in range(row_lines):
            mid[q, d] = (
                part[q, d, core].astype(jnp.float32) + first[q, d].astype(jnp.float32)
            ).astype(jnp.bfloat16)

    def rs_lines_start(w, q):
        for k in range(1, row_lines):
            rs_line(w, q, k).start()

    def rs_finish(w, q):
        result = mid[q, depth_me].astype(jnp.float32)
        for k in range(1, row_lines):
            rs_line(w, q, k).wait()
            result = result + second[q, k - 1].astype(jnp.float32)
        return result

    def square_copy(q, k):
        return remote(
            square_own.at[q],
            square_buf.at[q, k - 1],
            square_send.at[q, k - 1],
            square_recv.at[q, k - 1],
            "col",
            lax.rem(col + k, cols),
        )

    def stream_step(q):
        value = rs_finish(0, q) + res_ref[q].astype(jnp.float32)
        stream[q] = value
        squares = jnp.sum(value * value, axis=1, keepdims=True)
        square_own[q] = jnp.broadcast_to(squares, (toks, 128))
        for k in range(1, cols):
            square_copy(q, k).start()
        pieces[q, depth_me, core] = (value * gain_ref[...].astype(jnp.float32)[None, :]).astype(jnp.bfloat16)
        for k in range(1, row_lines):
            ag_line(q, k).start()
        ag_pair(q, 0).start()

    def ag_line(q, k):
        return remote(
            pieces.at[q, depth_me, core],
            pieces.at[q, depth_me, core],
            ag_line_send.at[q, k - 1],
            ag_line_recv.at[q, k - 1],
            "row",
            layer(k) * 2 + core,
        )

    def ag_pair(q, k):
        owner = layer(row_lines - k)
        return remote(
            pieces.at[q, owner, core],
            pieces.at[q, owner, core],
            ag_pair_send.at[q, k],
            ag_pair_recv.at[q, k],
            "row",
            row_other,
        )

    def factor_copy(q, k):
        return remote(
            factors.at[q, core],
            factors.at[q, core],
            factor_send.at[q, k - 1],
            factor_recv.at[q, core],
            "row",
            flipped(row, k),
        )

    def factor_step(q):
        squares = square_own[q]
        for k in range(1, cols):
            square_copy(q, k).wait()
            squares = squares + square_buf[q, k - 1]

        @pl.when(depth_me == col)
        def _():
            factors[q, core] = lax.rsqrt(squares / (width * cols) + 1e-05)
            for k in range(1, rows):
                factor_copy(q, k).start()

    def factor_wait(q):
        for c in range(2):

            @pl.when(row != 2 * col + c)
            def _():
                pltpu.make_async_copy(factors.at[q, c], factors.at[q, c], factor_recv.at[q, c]).wait()

    def factor_finish():
        @pl.when(depth_me == col)
        def _():
            for q in range(NC):
                for k in range(1, rows):
                    factor_copy(q, k).wait_send()

    def ag_forward(q):
        for k in range(1, row_lines):
            ag_line(q, k).wait()
            ag_pair(q, k).start()

    def ag_done(q):
        for k in range(row_lines):
            ag_pair(q, k).wait()

    def transfers(stage, step):
        slot = lax.rem(step, SLOTS)
        hold = lax.rem(step, HOLD)
        if stage == 0:
            pair = (gate_part.at[hold, 1 - pair_me], gate_first.at[slot])
            along = [(up_part.at[hold, line(k)], up_first.at[slot, k - 1]) for k in range(1, col_lines)]
        elif stage == 1:
            pair = (up_mid.at[hold, 1 - pair_me], up_second.at[slot])
            along = [(gate_mid.at[hold, line(k)], gate_second.at[slot, k - 1]) for k in range(1, col_lines)]
        elif stage == 2:
            pair = (left.at[slot, 0, 0], left.at[slot, 0, 1])
            along = [(right.at[slot, 0, 0], right.at[slot, 0, k]) for k in range(1, col_lines)]
        else:
            pair = (right.at[slot, 0], right.at[slot, 1])
            along = [(left.at[slot, 0], left.at[slot, k]) for k in range(1, col_lines)]
        copies = [
            remote(*pair, pair_send.at[stage, slot], pair_recv.at[stage, slot], "col", col_other)
        ]
        for k in range(1, col_lines):
            copies.append(
                remote(
                    *along[k - 1],
                    line_send.at[stage, slot, k - 1],
                    line_recv.at[stage, slot, k - 1],
                    "col",
                    line(k) * 2 + pair_me,
                )
            )
        return copies

    for p in range(spare):
        wo_copy(p).start()

    def begin():
        for j in range(steps):
            gate_copy(j).start()
            up_copy(j).start()
        for j in range(steps - spare):
            down_copy(j).start()

    finish = attention(
        rows,
        cols,
        local_blocks,
        begin,
        query_ref,
        block_ref,
        lists_ref,
        near_key_ref,
        near_value_ref,
        att_ref,
        held,
        near,
        turned,
        top,
        norm,
        acc,
        stats,
        near_sem,
        near_send,
        near_recv,
        block_send,
        block_recv,
        swap_send,
        swap_recv,
    )
    for q in range(NC):
        for k in range(1, cols):
            att_copy(q, k).start()
    total[...] = jnp.zeros_like(total)
    for p in range(spare):
        wo_copy(p).wait()

    def project(q):
        att_buf[q, col] = att_ref[:, q * toks : (q + 1) * toks, :]
        for k in range(1, cols):
            att_copy(q, k).wait()
        inputs = att_buf[q].reshape(many, att_buf.shape[-1])
        for start in range(0, width, tile):
            product = jnp.zeros((many, tile), jnp.float32)
            for p in range(spare):
                product = product + jnp.dot(
                    inputs[:, p * wide : (p + 1) * wide],
                    down_buf[steps - spare + p, :, start : start + tile],
                    preferred_element_type=jnp.float32,
                )
            part[q, :, :, :, start : start + tile] = product.astype(jnp.bfloat16).reshape(
                row_lines, 2, toks, tile
            )
        rs_pair(0, q).start()

    project(0)
    rs_middle(0, 0)
    rs_lines_start(0, 0)
    project(1)
    rs_middle(0, 1)
    rs_lines_start(0, 1)
    stream_step(0)
    stream_step(1)
    factor_step(0)
    for q in range(2, NC):
        project(q)
    for j in range(steps - spare, steps):
        down_copy(j).start()
    for q in range(2, NC):
        rs_middle(0, q)
    rs_lines_start(0, 2)
    factor_step(1)
    ag_forward(0)

    finish()
    chunks = NC * steps

    def stage_when(i, stage):
        return pl.when((i >= LAGS[stage]) & (i < chunks + LAGS[stage]))

    def iteration(i, carry):
        q_now = i // steps
        j_now = lax.rem(i, steps)

        @pl.when((j_now == 0) & (q_now < NC))
        def _():
            ag_done(q_now)

        @stage_when(i, 0)
        def _():
            @pl.when(i < steps)
            def _():
                gate_copy(i).wait()
                up_copy(i).wait()

            hold = lax.rem(i, HOLD)
            inputs = pieces[q_now].reshape(many, pieces.shape[-1])
            product = jnp.dot(inputs, gate_buf[j_now], preferred_element_type=jnp.float32).astype(jnp.bfloat16)
            for b in range(cols):
                gate_part[hold, b % 2, b // 2] = product[b * share : (b + 1) * share]
            product = jnp.dot(inputs, up_buf[j_now], preferred_element_type=jnp.float32).astype(jnp.bfloat16)
            for b in range(cols):
                up_part[hold, b // 2, b % 2] = product[b * share : (b + 1) * share]
            for copy in transfers(0, i):
                copy.start()

        @stage_when(i, 1)
        def _():
            step = i - LAGS[1]
            slot = lax.rem(step, SLOTS)
            hold = lax.rem(step, HOLD)
            for copy in transfers(0, step):
                copy.wait()
            gate_mid[hold] = (
                gate_part[hold, pair_me].astype(jnp.float32) + gate_first[slot].astype(jnp.float32)
            ).astype(jnp.bfloat16)
            up_sum = up_part[hold, line_me].astype(jnp.float32)
            for k in range(1, col_lines):
                up_sum = up_sum + up_first[slot, k - 1].astype(jnp.float32)
            up_mid[hold] = up_sum.astype(jnp.bfloat16)
            for copy in transfers(1, step):
                copy.start()

        @stage_when(i, 2)
        def _():
            step = i - LAGS[2]
            slot = lax.rem(step, SLOTS)
            hold = lax.rem(step, HOLD)
            for copy in transfers(1, step):
                copy.wait()
            gate = gate_mid[hold, line_me].astype(jnp.float32)
            for k in range(1, col_lines):
                gate = gate + gate_second[slot, k - 1].astype(jnp.float32)
            up = up_mid[hold, pair_me].astype(jnp.float32) + up_second[slot].astype(jnp.float32)
            q = step // steps

            @pl.when(lax.rem(step, steps) == 0)
            def _():
                factor_wait(q)

            factor = factors[q].reshape(share, 128)[:, :1]
            gate = gate * factor
            hidden = (gate / (1.0 + jnp.exp(-gate)) * (up * factor)).astype(jnp.bfloat16)
            left[slot, 0, 0] = hidden[:, :half]
            right[slot, 0, 0] = hidden[:, half:]
            for copy in transfers(2, step):
                copy.start()

        @stage_when(i, 3)
        def _():
            for copy in transfers(2, i - LAGS[3]):
                copy.wait()
            for copy in transfers(3, i - LAGS[3]):
                copy.start()

        @stage_when(i, 4)
        def _():
            step = i - LAGS[4]
            j = lax.rem(step, steps)
            slot = lax.rem(step, SLOTS)

            @pl.when(step < steps)
            def _():
                down_copy(step).wait()

            for copy in transfers(3, step):
                copy.wait()
            gathered = jnp.concatenate(
                [
                    jnp.concatenate([left[slot, k, p], right[slot, p, k]], axis=1)
                    for p in range(2)
                    for k in range(col_lines)
                ],
                axis=0,
            )
            for start in range(0, width, tile):
                total[:, start : start + tile] += jnp.dot(
                    gathered,
                    down_buf[j, :, start : start + tile],
                    preferred_element_type=jnp.float32,
                )

        @pl.when((j_now == 5) & (q_now + 2 < NC))
        def _():
            stream_step(q_now + 2)

        @pl.when((j_now == 6) & (q_now + 2 < NC))
        def _():
            factor_step(q_now + 2)

        @pl.when((j_now == 5) & (q_now + 3 < NC))
        def _():
            rs_lines_start(0, q_now + 3)

        @pl.when((j_now == 5) & (q_now + 1 < NC))
        def _():
            ag_forward(q_now + 1)

        done = i - LAGS[4] + 1
        q_done = done // steps - 1

        @pl.when((done > 0) & (lax.rem(done, steps) == 0))
        def _():
            for p in range(2):
                for k in range(col_lines):
                    owner = line(col_lines - k) * 2 + lax.rem(pair_me + p, 2)
                    begin = (p * col_lines + k) * share
                    part[q_done, owner] = (
                        total[begin : begin + share, :].astype(jnp.bfloat16).reshape(2, toks, width)
                    )
            rs_pair(1, q_done).start()
            total[...] = jnp.zeros_like(total)

        @pl.when((done > steps) & (lax.rem(done, steps) == 1))
        def _():
            rs_middle(1, q_done)
            rs_lines_start(1, q_done)

        @pl.when((done > steps) & (lax.rem(done, steps) == 5))
        def _():
            out_ref[q_done] = stream[q_done] + rs_finish(1, q_done)

        return carry

    lax.fori_loop(0, chunks + LAGS[4], iteration, 0)
    factor_finish()
    rs_middle(1, NC - 1)
    rs_lines_start(1, NC - 1)
    out_ref[NC - 1] = stream[NC - 1] + rs_finish(1, NC - 1)


def layer_call(
    queries,
    blocks,
    block_lists,
    local_blocks,
    stretch_keys,
    stretch_values,
    out_weight,
    residual,
    norm_gain,
    gate_weight,
    up_weight,
    down_weight,
):
    cols = lax.axis_size("col")
    rows = lax.axis_size("row")
    depth, hidden_width = gate_weight.shape
    tokens, width = residual.shape
    inner = out_weight.shape[0]
    wide = hidden_width // STEPS
    toks = tokens // NC
    share = rows * toks // cols
    col_lines = cols // 2
    row_lines = rows // 2
    devices = rows * cols
    lines = BLK * inner // HEAD_DIM
    assert rows == 2 * cols and inner % wide == 0
    vmem = pl.BlockSpec(memory_space=pltpu.VMEM)
    hbm = pl.BlockSpec(memory_space=pl.ANY)
    dma = pltpu.SemaphoreType.DMA

    def held(*shape):
        return pltpu.VMEM(shape, jnp.bfloat16)

    out = pl.pallas_call(
        functools.partial(layer_kernel, cols, rows, local_blocks),
        out_shape=jax.ShapeDtypeStruct((NC, toks, width), jnp.float32),
        in_specs=[vmem, hbm, vmem, hbm, hbm, hbm, vmem, vmem, hbm, hbm, hbm],
        out_specs=vmem,
        scratch_shapes=[
            held(STEPS, depth, wide),
            held(STEPS, depth, wide),
            held(STEPS, wide, width),
            held(devices, 2, BLK, HEAD_DIM),
            held(cols, 2, BLK, HEAD_DIM),
            held(3, HEAD_DIM, lines),
            pltpu.VMEM((2, 1, lines), jnp.float32),
            pltpu.VMEM((2, 1, lines), jnp.float32),
            pltpu.VMEM((2, HEAD_DIM, lines), jnp.float32),
            pltpu.VMEM((2, 2, lines), jnp.float32),
            held(BLK // tokens, tokens, inner),
            held(NC, cols, 2, toks, inner),
            held(NC, row_lines, 2, toks, width),
            held(NC, row_lines, toks, width),
            held(NC, row_lines, toks, width),
            held(NC, row_lines - 1, toks, width),
            pltpu.VMEM((NC, toks, width), jnp.float32),
            pltpu.VMEM((NC, toks, 128), jnp.float32),
            pltpu.VMEM((NC, cols - 1, toks, 128), jnp.float32),
            pltpu.VMEM((NC, 2, toks, 128), jnp.float32),
            held(NC, row_lines, 2, toks, depth),
            held(HOLD, 2, col_lines, share, wide),
            held(HOLD, col_lines, 2, share, wide),
            held(SLOTS, col_lines, share, wide),
            held(SLOTS, col_lines - 1, 2, share, wide),
            held(HOLD, col_lines, share, wide),
            held(HOLD, 2, share, wide),
            held(SLOTS, col_lines - 1, share, wide),
            held(SLOTS, share, wide),
            held(SLOTS, col_lines, 2, share, wide // 2),
            held(SLOTS, 2, col_lines, share, wide // 2),
            pltpu.VMEM((cols * share, width), jnp.float32),
            dma((STEPS,)),
            dma((STEPS,)),
            dma((STEPS,)),
            dma((inner // wide,)),
            dma((2,)),
            dma((cols - 1,)),
            dma((cols - 1,)),
            dma((devices,)),
            dma((devices,)),
            dma((3,)),
            dma((3,)),
            dma((NC, cols - 1)),
            dma((NC, cols - 1)),
            dma((2, NC)),
            dma((2, NC)),
            dma((2, NC, row_lines - 1)),
            dma((2, NC, row_lines - 1)),
            dma((NC, cols - 1)),
            dma((NC, cols - 1)),
            dma((NC, rows - 1)),
            dma((NC, 2)),
            dma((NC, row_lines - 1)),
            dma((NC, row_lines - 1)),
            dma((NC, row_lines)),
            dma((NC, row_lines)),
            dma((4, SLOTS)),
            dma((4, SLOTS)),
            dma((4, SLOTS, col_lines - 1)),
            dma((4, SLOTS, col_lines - 1)),
        ],
        compiler_params=pltpu.CompilerParams(
            collective_id=0, has_side_effects=True, vmem_limit_bytes=67 * 1000 * 1000
        ),
    )(
        queries,
        blocks,
        block_lists,
        stretch_keys,
        stretch_values,
        out_weight,
        residual.reshape(NC, toks, width),
        norm_gain,
        gate_weight,
        up_weight,
        down_weight,
    )
    return out.reshape(tokens, width).astype(jnp.bfloat16)


def local(
    queries,
    cache_keys,
    cache_values,
    stretch_keys,
    stretch_values,
    block_lists,
    out_weight,
    residual,
    norm_gain,
    gate_weight,
    up_weight,
    down_weight,
):
    row_count = lax.axis_size("row")
    col_count = lax.axis_size("col")
    row_index = lax.axis_index("row")
    col_index = lax.axis_index("col")
    device_count = row_count * col_count
    my_index = row_index * col_count + col_index
    local_blocks = cache_keys.shape[1] // BLK
    within = block_lists - my_index * local_blocks
    matched = (within >= 0) & (within < local_blocks)
    block_rows = jnp.sum(jnp.where(matched, within, 0), axis=2)
    blocks = gather_blocks(block_rows, cache_keys, cache_values, device_count)
    return layer_call(
        queries,
        blocks,
        block_lists,
        local_blocks,
        stretch_keys,
        stretch_values,
        out_weight,
        residual,
        norm_gain,
        gate_weight,
        up_weight,
        down_weight,
    )


def solution(mesh):
    in_specs = (
        P("col", "row"),
        P(None, ("row", "col"), None),
        P(None, ("row", "col"), None),
        P(None, "col", None),
        P(None, "col", None),
        P(),
        P("row", "col"),
        P("row", "col"),
        P("col"),
        P("col", "row"),
        P("col", "row"),
        P("row", "col"),
    )
    out_specs = P("row", "col")
    return jax.shard_map(local, mesh=mesh, in_specs=in_specs, out_specs=out_specs, check_vma=False)
```
